32 devices in a mesh: wide: 16 (over z, y, x), clus: 2 (over core).
Axes of the slice: x: 2, y: 2, z: 4, core: 2. Of those that a mesh axis runs over, the one named last changes fastest.
Arguments:
- duals: bfloat16 [96, 64, 3840], P(None, ('wide', 'clus')), may hold values from -6 to 6
- kernel: bfloat16 [64, 6, 3840], P(('wide', 'clus')), may hold values from -0.29882812 to 0.29882812
- sub_counts: int32 [32], P(('wide', 'clus')), may hold values from 1 to 2, as said below
- dual_sizes: int32 [64], P(('wide', 'clus')), may hold values from 1920 to 3840, as said below
- cluster_factor: float32 [16, 24, 24], P('wide'), as said below
- coarse_map: int32 [16, 24], P('wide'), may hold values from 0 to 383, as said below
- coarse_inverse: float32 [384, 384], P(None, 'clus'), as said below
Outputs:
- projected: bfloat16 [96, 64, 3840], P(None, ('wide', 'clus'))
The draws below stay inside these ranges and needn't reach their ends.
Inputs may be any that keep to these rules, and one draw needn't show every extreme that they name: `sub_counts`: each device holds 1 to 2 subdomains; some device holds 2. `dual_sizes`: some slot has the full 3840. `coarse_map`: the rows of cluster w map into the 48 global rows that begin at w * 24, counted modulo 384. `cluster_factor`: lower triangular with diagonal entries between 1 and 2. `coarse_inverse`: diagonal entries between 1 and 2.
All inputs are finite; a program needn't handle non-finite values.
Results may differ from the reference program's by a relative error of at most 0.0018.
Values sent between devices are 32-bit elements; how exact they have to be, the bound alone decides.
No kernel may reach another device: no remote copies, remote signals or barrier semaphores. Data moves between devices by JAX's collectives and lax.ppermute only.
A program may use at most 64 MiB of HBM per device.

```python
import math
import jax
import jax.numpy as jnp
from jax import lax

DUAL = 3840
MODES = 6
SUB = 2
RHS = 96
BAND = 24
DEVS = 32
NSUB = 64
CK = 24
GK = 384
N_WIDE = 16
N_CLUS = 2


def draw_sub_counts(key, part):
    first_key, second_key = jax.random.split(key)
    values = jax.random.randint(first_key, (DEVS,), 1, SUB + 1)
    where_full = jax.random.randint(second_key, (), 0, DEVS)
    return values.at[where_full].set(SUB).astype(jnp.int32)


def draw_dual_sizes(key, part):
    first_key, second_key = jax.random.split(key)
    values = jax.random.randint(first_key, (NSUB,), DUAL // 2, DUAL + 1)
    where_full = jax.random.randint(second_key, (), 0, NSUB)
    return values.at[where_full].set(DUAL).astype(jnp.int32)


def draw_coarse_map(key, part):
    clusters = GK // BAND
    offsets = jax.random.randint(key, (clusters, CK), 0, 2 * BAND)
    base_rows = jnp.arange(clusters, dtype=jnp.int32)[:, None] * BAND
    mapped = (base_rows + offsets) % GK
    mapped = mapped.at[:, 0].set(base_rows[:, 0] + BAND - 1)
    mapped = mapped.at[:, 1].set(base_rows[:, 0])
    return mapped.astype(jnp.int32)


def draw_cluster_factor(key, part):
    clusters = GK // BAND
    first_key, second_key = jax.random.split(key)
    diag_vals = jnp.exp(jax.random.uniform(first_key, (clusters, CK), jnp.float32, 0.0, math.log(2.0)))
    off_vals = jax.random.uniform(second_key, (clusters, CK, CK), jnp.float32, -1.0, 1.0) * (0.8 / math.sqrt(CK))
    identity = jnp.eye(CK, dtype=jnp.float32)
    return (jnp.tril(off_vals, -1) + identity[None, :, :] * diag_vals[:, :, None]).astype(jnp.float32)


def draw_coarse_inverse(key, part):
    first_key, second_key = jax.random.split(key)
    diag_vals = jnp.exp(jax.random.uniform(first_key, (GK,), jnp.float32, 0.0, math.log(2.0)))
    off_vals = jax.random.uniform(second_key, (GK, GK), jnp.float32, -1.0, 1.0) * (0.8 / math.sqrt(GK))
    identity = jnp.eye(GK, dtype=jnp.float32)
    return (off_vals * (1.0 - identity) + identity * diag_vals[:, None]).astype(jnp.float32)


def levels(key, dims, pieces, smallest, largest):
    gain = 1.0
    for dim, parts in pieces:
        steps = jax.random.uniform(jax.random.fold_in(jax.random.fold_in(key, 6), dim), (parts,), jnp.float32, smallest / len(pieces), largest / len(pieces))
        gain = gain * jnp.repeat(jnp.exp(steps), dims[dim] // parts).reshape((-1,) + (1,) * (len(dims) - 1 - dim))
    return gain


def normal_values(stream_key, shape, width, bound, cuts=(), kind=jnp.bfloat16):
    factor_of = levels(stream_key, shape, cuts, -0.22, 0.18) if cuts else 1.0
    result = jax.random.normal(stream_key, shape, jnp.float32) * width * factor_of
    return jnp.minimum(jnp.maximum(result, -bound), bound).astype(kind)


def setup_inputs(seed: int = 0) -> dict:
    arg_keys = jax.random.split(jax.random.key(seed), 8)
    duals = normal_values(arg_keys[0], (RHS, NSUB, DUAL), 1.0, 6.0, ((1, 32),))
    kernel = normal_values(arg_keys[1], (NSUB, MODES, DUAL), 0.05, 0.29882812, ((0, 32),))
    sub_counts = draw_sub_counts(jax.random.fold_in(arg_keys[7], 71), 0)
    dual_sizes = draw_dual_sizes(jax.random.fold_in(arg_keys[7], 71), 0)
    cluster_factor = draw_cluster_factor(jax.random.fold_in(arg_keys[7], 71), 0)
    coarse_map = draw_coarse_map(jax.random.fold_in(arg_keys[7], 71), 0)
    coarse_inverse = draw_coarse_inverse(jax.random.fold_in(arg_keys[7], 71), 0)
    return dict(duals=duals, kernel=kernel, sub_counts=sub_counts, dual_sizes=dual_sizes, cluster_factor=cluster_factor, coarse_map=coarse_map, coarse_inverse=coarse_inverse)


def masked_kernel(kernel, sub_counts, dual_sizes):
    total = kernel.shape[0]
    position = lax.broadcasted_iota(jnp.int32, (total, DUAL), 1)
    slot_index = lax.broadcasted_iota(jnp.int32, (total, DUAL), 0)
    owner_count = sub_counts[slot_index // SUB]
    active = (position < dual_sizes[:, None]) & (slot_index % SUB < owner_count)
    return jnp.where(active[:, None, :], kernel, jnp.zeros_like(kernel)).astype(jnp.bfloat16)

def reference(duals, kernel, sub_counts, dual_sizes, cluster_factor, coarse_map, coarse_inverse):
    masked = masked_kernel(kernel, sub_counts, dual_sizes)
    per_cluster = SUB * N_CLUS
    hi = lax.Precision.HIGHEST

    def first(cluster):
        block = lax.dynamic_slice_in_dim(duals, cluster * per_cluster, per_cluster, 1)
        kblock = lax.dynamic_slice_in_dim(masked, cluster * per_cluster, per_cluster, 0)
        local = jnp.einsum('rsi,ski->rsk', block.astype(jnp.float32), kblock.astype(jnp.float32), precision=hi)
        local = local.reshape(RHS, CK)
        return lax.linalg.triangular_solve(cluster_factor[cluster], local.T, left_side=True, lower=True).T
    forward = lax.map(first, jnp.arange(N_WIDE, dtype=jnp.int32))
    flat = jnp.transpose(forward, (0, 2, 1)).reshape(N_WIDE * CK, RHS)
    gsum = jax.ops.segment_sum(flat, coarse_map.reshape(-1), num_segments=GK).T
    beta = jnp.dot(gsum, coarse_inverse, precision=hi)

    def second(cluster):
        block = lax.dynamic_slice_in_dim(duals, cluster * per_cluster, per_cluster, 1)
        kblock = lax.dynamic_slice_in_dim(masked, cluster * per_cluster, per_cluster, 0)
        back = beta[:, coarse_map[cluster]]
        corr = lax.linalg.triangular_solve(cluster_factor[cluster], (forward[cluster] - back).T, left_side=True, lower=True, transpose_a=True).T
        corr = corr.reshape(RHS, per_cluster, MODES).astype(jnp.bfloat16)
        delta = jnp.einsum('rsk,ski->rsi', corr.astype(jnp.float32), kblock.astype(jnp.float32), precision=hi)
        return (block.astype(jnp.float32) - delta).astype(jnp.bfloat16)
    blocks = lax.map(second, jnp.arange(N_WIDE, dtype=jnp.int32))
    return jnp.transpose(blocks, (1, 0, 2, 3)).reshape(RHS, NSUB, DUAL)
```

```python
import jax
import jax.numpy as jnp
from jax import lax
from jax.sharding import PartitionSpec as P


def per_device(duals, kernel, sub_counts, dual_sizes, cluster_factor, coarse_map, coarse_inverse):
    rhs_count, sub_count, dual_width = duals.shape
    mode_count = kernel.shape[1]
    hi = lax.Precision.HIGHEST
    position = lax.broadcasted_iota(jnp.int32, (sub_count, dual_width), 1)
    slot_index = lax.broadcasted_iota(jnp.int32, (sub_count, dual_width), 0)
    active = (position < dual_sizes[:, None]) & (slot_index < sub_counts[0])
    masked = jnp.where(active[:, None, :], kernel, jnp.zeros_like(kernel))
    local = jnp.einsum("rsi,ski->rsk", duals, masked, preferred_element_type=jnp.float32)
    local = local.reshape(rhs_count, sub_count * mode_count)
    cluster_vec = lax.all_gather(local, "clus", axis=1, tiled=True)
    lower = cluster_factor[0]
    rows_map = coarse_map[0]
    cluster_rows = rows_map.shape[0]
    global_rows = coarse_inverse.shape[0]
    clusters = lax.axis_size("wide")
    forward = lax.linalg.triangular_solve(lower, cluster_vec.T, left_side=True, lower=True)
    payload = jnp.concatenate([forward, rows_map.astype(jnp.float32)[:, None]], axis=1)
    spread = jnp.broadcast_to(payload[None], (clusters,) + payload.shape)
    gathered = lax.all_to_all(spread, "wide", 0, 0).reshape(clusters * cluster_rows, rhs_count + 1)
    all_forward = gathered[:, :rhs_count]
    all_map = gathered[:, rhs_count].astype(jnp.int32)
    all_hot = (
        all_map[:, None] == lax.broadcasted_iota(jnp.int32, (clusters * cluster_rows, global_rows), 1)
    ).astype(jnp.float32)
    gsum = lax.dot_general(all_forward, all_hot, (((0,), (0,)), ((), ())), precision=hi)
    beta_part = jnp.dot(gsum, coarse_inverse, precision=hi)
    beta = lax.all_gather(beta_part, "clus", axis=1, tiled=True)
    one_hot = (
        rows_map[:, None] == lax.broadcasted_iota(jnp.int32, (cluster_rows, global_rows), 1)
    ).astype(jnp.float32)
    back = jnp.dot(one_hot, beta.T, precision=hi)
    corr = lax.linalg.triangular_solve(
        lower, forward - back, left_side=True, lower=True, transpose_a=True
    )
    own_rows = lax.dynamic_slice_in_dim(
        corr, lax.axis_index("clus") * sub_count * mode_count, sub_count * mode_count, 0
    )
    own_corr = own_rows.T.reshape(rhs_count, sub_count, mode_count).astype(jnp.bfloat16)
    delta = jnp.einsum("rsk,ski->rsi", own_corr, masked, preferred_element_type=jnp.float32)
    return (duals.astype(jnp.float32) - delta).astype(jnp.bfloat16)


def solution(mesh):
    in_specs = (
        P(None, ("wide", "clus"), None),
        P(("wide", "clus"), None, None),
        P(("wide", "clus")),
        P(("wide", "clus")),
        P("wide", None, None),
        P("wide", None),
        P(None, "clus"),
    )
    out_specs = P(None, ("wide", "clus"), None)
    return jax.shard_map(
        per_device, mesh=mesh, in_specs=in_specs, out_specs=out_specs, check_vma=False
    )
```

```python
import functools

import jax
import jax.numpy as jnp
from jax import lax
from jax.experimental import pallas as pl
from jax.experimental.pallas import tpu as pltpu
from jax.sharding import PartitionSpec as P

F32 = jnp.float32
BF16 = jnp.bfloat16
LANES = 128
HI = lax.Precision.HIGHEST
NT = (((1,), (1,)), ((), ()))
NN = (((1,), (0,)), ((), ()))
VMEM = pl.BlockSpec(memory_space=pltpu.VMEM)
HBM = pl.BlockSpec(memory_space=pltpu.HBM)
FIRST_LIMIT = 60 * 2**20
LAST_LIMIT = 20 * 2**20


def iota(shape, dim):
    return lax.broadcasted_iota(jnp.int32, shape, dim)


def split(x, parts):
    out = []
    for n in range(parts):
        head = x.astype(BF16)
        out.append(head)
        if n + 1 < parts:
            x = x - head.astype(F32)
    return out


def dot(a, b, dims):
    return lax.dot_general(a, b, dims, preferred_element_type=F32)


def chunks_of(width):
    for count in (5, 3, 2):
        if width % (count * LANES) == 0:
            return count
    return 1


def rows_of_slots(sub, rhs, lanes):
    return (iota((rhs * sub, lanes), 0) // sub == iota((rhs * sub, lanes), 1)).astype(F32).astype(BF16)


def first_kernel(rhs, counts_ref, sizes_ref, kernel_ref, lower_ref, map_ref, duals_ref,
                 send_ref, masked_ref, inv_ref,
                 count_s, size_s, raw_ref, tri_ref, row_ref, x_ref, acc_ref, sol_ref, own_ref, sems, small_sems):
    modes, sub, width = kernel_ref.shape
    rows = modes * sub
    ck = lower_ref.shape[0]
    lanes = inv_ref.shape[1]
    count = chunks_of(width)
    step = width // count

    def copy(n):
        cols = pl.ds(n * step, step)
        return pltpu.make_async_copy(duals_ref.at[:, :, cols], x_ref.at[:, :, cols], sems.at[n])

    small = [
        pltpu.make_async_copy(src, dst, small_sems.at[n])
        for n, (src, dst) in enumerate(
            ((lower_ref, tri_ref), (map_ref, row_ref), (counts_ref, count_s), (sizes_ref, size_s), (kernel_ref, raw_ref))
        )
    ]
    for one in small:
        one.start()
    for n in range(count):
        copy(n).start()

    place = lax.axis_index("clus").astype(jnp.int32)
    small[0].wait()
    small[1].wait()
    upper = tri_ref[...].T
    sol = (iota((ck, lanes), 1) == rhs + iota((ck, lanes), 0)).astype(F32)
    row_id = iota((ck, 1), 0)
    for i in range(ck - 1, -1, -1):
        column = upper[:, i : i + 1]
        row = sol[i : i + 1, :] / upper[i : i + 1, i : i + 1]
        sol = jnp.where(row_id == i, row, sol - jnp.where(row_id < i, column, 0.0) * row)
    for c in range(lanes // LANES):
        cols = slice(c * LANES, (c + 1) * LANES)
        sol_ref[c] = sol[:, cols]
        for s in range(sub):
            own_ref[c, pl.ds(s, modes, stride=sub), :] = sol_ref[c, pl.ds(place * rows + s * modes, modes), :]
        inv_ref[:, cols] = own_ref[c]
    wanted = iota((rows, ck), 1) == place * rows + iota((rows, ck), 0)
    own_map = jnp.sum(jnp.where(wanted, row_ref[...].astype(F32), 0.0), axis=1, keepdims=True)

    for one in small[2:]:
        one.wait()
    slot = iota((rows, width), 0) % sub
    limit = jnp.zeros((rows, width), jnp.int32)
    for s in range(sub):
        size = jnp.where(s < count_s[0], size_s[s], 0)
        limit = jnp.where(slot == s, size, limit)
    values = raw_ref[...].reshape(rows, width).astype(F32)
    masked_ref[...] = jnp.where(iota((rows, width), 1) < limit, values, 0.0).astype(BF16)

    acc_ref[...] = jnp.zeros_like(acc_ref)
    for n in range(count):
        copy(n).wait()
        x = x_ref[:, :, n * step : (n + 1) * step].reshape(rhs * sub, step)
        acc_ref[...] += dot(masked_ref[:, n * step : (n + 1) * step], x, NT)
    same = iota((rows, rhs * sub), 0) % sub == iota((rows, rhs * sub), 1) % sub
    mixed = jnp.where(same, acc_ref[...], 0.0)
    pick = rows_of_slots(sub, rhs, lanes)
    local = sum(dot(part, pick, NN) for part in split(mixed, 3))
    block = local + inv_ref[...] + jnp.where(iota((rows, lanes), 1) == rhs + ck, own_map, 0.0)
    group = 2 if send_ref.shape[0] % (2 * rows) == 0 else 1
    block = jnp.concatenate([block] * group, axis=0)
    for d in range(send_ref.shape[0] // (rows * group)):
        send_ref[pl.ds(d * rows * group, rows * group), :] = block


def write_out(corr, masked_ref, x_ref, out_ref, o_ref, sems):
    rhs, sub, width = x_ref.shape
    rows = masked_ref.shape[0]
    count = chunks_of(width)
    step = width // count
    pick = rows_of_slots(sub, rhs, rhs)
    wide = dot(pick, corr, NT)
    same = iota((rhs * sub, rows), 0) % sub == iota((rhs * sub, rows), 1) % sub
    wide = jnp.where(same, wide, 0.0).astype(BF16)

    def copy(n):
        cols = pl.ds(n * step, step)
        return pltpu.make_async_copy(o_ref.at[:, :, cols], out_ref.at[:, :, cols], sems.at[n])

    for n in range(count):
        cols = slice(n * step, (n + 1) * step)
        x = x_ref[:, :, cols].reshape(rhs * sub, step).astype(F32)
        value = x - dot(wide, masked_ref[:, cols], NN)
        o_ref[:, :, cols] = value.astype(BF16).reshape(rhs, sub, step)
        copy(n).start()
    for n in range(count):
        copy(n).wait()


def last_kernel(rhs, ck, recv_ref, coarse_ref, own_ref, masked_ref, x_ref, out_ref, o_ref, block_ref, sems):
    total = recv_ref.shape[0]
    gk = coarse_ref.shape[1]
    target = recv_ref[:, rhs + ck : rhs + ck + 1].astype(jnp.int32)
    hot = (target == iota((total, gk), 1)).astype(F32).astype(BF16)
    taken = sum(dot(part, hot, NT) for part in split(coarse_ref[...], 3))
    block_ref[...] = jnp.zeros_like(block_ref)
    for w in range(total // ck):
        here = slice(w * ck, (w + 1) * ck)
        block_ref[here, here] = recv_ref[here, rhs : rhs + ck]
    left = own_ref[...] - taken
    left_hi, left_lo = split(left, 2)
    block_hi, block_lo = split(block_ref[...], 2)
    weight = dot(left_hi, block_hi, NT) + dot(left_lo, block_hi, NT) + dot(left_hi, block_lo, NT)
    weight_hi, weight_lo = split(weight, 2)
    local_hi, local_lo = split(recv_ref[:, :rhs], 2)
    corr = dot(weight_hi, local_hi, NN) + dot(weight_lo, local_hi, NN) + dot(weight_hi, local_lo, NN)
    write_out(corr.astype(BF16), masked_ref, x_ref, out_ref, o_ref, sems)


def last_kernel_plain(corr_ref, masked_ref, x_ref, out_ref, o_ref, sems):
    write_out(corr_ref[...].astype(BF16), masked_ref, x_ref, out_ref, o_ref, sems)


def per_device(duals, kernel, sub_counts, dual_sizes, cluster_factor, coarse_map, coarse_inverse):
    rhs, sub, width = duals.shape
    modes = kernel.shape[1]
    rows = sub * modes
    clusters = lax.axis_size("wide")
    members = lax.axis_size("clus")
    devices = clusters * members
    total = devices * rows
    ck = cluster_factor.shape[1]
    gk, own_cols = coarse_inverse.shape
    lanes = -(-(rhs + ck + 1) // LANES) * LANES
    count = chunks_of(width)
    place = lax.axis_index("clus").astype(jnp.int32)
    params = pltpu.CompilerParams(vmem_limit_bytes=LAST_LIMIT)

    send, masked, inv = pl.pallas_call(
        functools.partial(first_kernel, rhs),
        out_shape=(
            jax.ShapeDtypeStruct((total, lanes), F32),
            jax.ShapeDtypeStruct((rows, width), BF16),
            jax.ShapeDtypeStruct((rows, lanes), F32),
        ),
        in_specs=[HBM] * 6,
        out_specs=(VMEM, VMEM, VMEM),
        scratch_shapes=[
            pltpu.SMEM((1,), jnp.int32),
            pltpu.SMEM((sub,), jnp.int32),
            pltpu.VMEM((modes, sub, width), BF16),
            pltpu.VMEM((ck, ck), F32),
            pltpu.VMEM((1, ck), jnp.int32),
            pltpu.VMEM((rhs, sub, width), BF16),
            pltpu.VMEM((rows, rhs * sub), F32),
            pltpu.VMEM((lanes // LANES, ck, LANES), F32),
            pltpu.VMEM((lanes // LANES, rows, LANES), F32),
            pltpu.SemaphoreType.DMA((count,)),
            pltpu.SemaphoreType.DMA((5,)),
        ],
        compiler_params=pltpu.CompilerParams(vmem_limit_bytes=FIRST_LIMIT),
    )(sub_counts, dual_sizes, kernel.transpose(1, 0, 2), cluster_factor[0], coarse_map, duals)

    spread = send.reshape(devices, rows, lanes // LANES, LANES)
    recv = lax.all_to_all(spread, ("wide", "clus"), 0, 0)

    inv, rows_map, coarse_t, _ = lax.optimization_barrier((inv, coarse_map[0], coarse_inverse.T, send))
    hot = (rows_map[:, None] == place * own_cols + iota((ck, own_cols), 1)).astype(F32)
    part = jnp.dot(hot, coarse_t, precision=HI)
    picked = part
    for shift in range(1, members):
        picked = picked + lax.ppermute(part, "clus", [(i, (i + shift) % members) for i in range(members)])
    own_inv = inv[:, rhs : rhs + ck]
    coarse = jnp.dot(own_inv, picked, precision=HI)

    scratch = pltpu.VMEM((rhs, sub, width), BF16)
    sems = pltpu.SemaphoreType.DMA((count,))
    out_shape = jax.ShapeDtypeStruct(duals.shape, BF16)
    if total * max(total, gk) <= 2**20:
        cluster = iota((1, clusters, 1), 1) == lax.axis_index("wide")
        own = jnp.where(cluster, own_inv[:, None, :], 0.0).reshape(rows, total)
        return pl.pallas_call(
            functools.partial(last_kernel, rhs, ck),
            out_shape=out_shape,
            in_specs=[VMEM] * 5,
            out_specs=HBM,
            scratch_shapes=[scratch, pltpu.VMEM((total, total), F32), sems],
            compiler_params=params,
        )(recv.reshape(total, lanes), coarse, own, masked, duals)

    blocks = recv.reshape(clusters, ck, lanes)
    forward = jnp.einsum("wma,wmr->war", blocks[:, :, rhs : rhs + ck], blocks[:, :, :rhs], precision=HI)
    target = blocks[:, :, rhs + ck].astype(jnp.int32).reshape(total)
    all_hot = (target[:, None] == iota((total, gk), 1)).astype(F32)
    gsum = lax.dot_general(all_hot, forward.reshape(total, rhs), (((0,), (0,)), ((), ())), precision=HI)
    mine = lax.dynamic_index_in_dim(forward, lax.axis_index("wide"), 0, keepdims=False)
    corr = jnp.dot(own_inv, mine, precision=HI) - jnp.dot(coarse, gsum, precision=HI)
    return pl.pallas_call(
        last_kernel_plain,
        out_shape=out_shape,
        in_specs=[VMEM] * 3,
        out_specs=HBM,
        scratch_shapes=[scratch, sems],
        compiler_params=params,
    )(corr, masked, duals)


def solution(mesh):
    in_specs = (
        P(None, ("wide", "clus"), None),
        P(("wide", "clus"), None, None),
        P(("wide", "clus")),
        P(("wide", "clus")),
        P("wide", None, None),
        P("wide", None),
        P(None, "clus"),
    )
    out_specs = P(None, ("wide", "clus"), None)
    return jax.shard_map(
        per_device, mesh=mesh, in_specs=in_specs, out_specs=out_specs, check_vma=False
    )
```

```python
import functools

import jax
import jax.numpy as jnp
from jax import lax
from jax.experimental import pallas as pl
from jax.experimental.pallas import tpu as pltpu
from jax.sharding import PartitionSpec as P

F32 = jnp.float32
BF16 = jnp.bfloat16
LANES = 128
HI = lax.Precision.HIGHEST
NT = (((1,), (1,)), ((), ()))
NN = (((1,), (0,)), ((), ()))
VMEM = pl.BlockSpec(memory_space=pltpu.VMEM)
HBM = pl.BlockSpec(memory_space=pltpu.HBM)
FIRST_LIMIT = 60 * 2**20
LAST_LIMIT = 20 * 2**20


def iota(shape, dim):
    return lax.broadcasted_iota(jnp.int32, shape, dim)


def stay(x):
    return pltpu.with_memory_space_constraint(x, pltpu.HBM)


def up(value, step):
    return -(-value // step) * step


def split(x, parts):
    out = []
    for n in range(parts):
        head = x.astype(BF16)
        out.append(head)
        if n + 1 < parts:
            x = x - head.astype(F32)
    return out


def dot(a, b, dims):
    return lax.dot_general(a, b, dims, preferred_element_type=F32)


def dot_parts(a, b, dims):
    a_hi, a_lo = split(a, 2)
    b_hi, b_lo = split(b, 2)
    rows = a.shape[0]
    both = dot(jnp.concatenate([a_hi, a_lo], axis=0), b_hi, dims)
    return both[:rows] + both[rows:] + dot(a_hi, b_lo, dims)


def dot_exact(a, hot, dims):
    rows = a.shape[0]
    parts = dot(jnp.concatenate(split(a, 3), axis=0), hot, dims)
    return parts[:rows] + parts[rows : 2 * rows] + parts[2 * rows :]


def chunks_of(width):
    for count in (5, 3, 2):
        if width % (count * LANES) == 0:
            return count
    return 1


def rows_of_slots(sub, rhs, lanes):
    return (iota((rhs * sub, lanes), 0) // sub == iota((rhs * sub, lanes), 1)).astype(F32).astype(BF16)


def slab_copies(whole_ref, slabs_ref, sems, back=False):
    count, rows, step = slabs_ref.shape
    flat = whole_ref.reshape(rows, count * step)

    def copy(n):
        part = flat.at[:, pl.ds(n * step, step)]
        ends = (slabs_ref.at[n], part) if back else (part, slabs_ref.at[n])
        return pltpu.make_async_copy(*ends, sems.at[n])

    return copy


def mask_kernel(raw_ref, count_s, size_s, sub):
    rows, width = raw_ref.shape
    slot = iota((rows, width), 0) % sub
    limit = jnp.zeros((rows, width), jnp.int32)
    for s in range(sub):
        size = jnp.where(s < count_s[0, 0], size_s[s], 0)
        limit = jnp.where(slot == s, size, limit)
    return jnp.where(iota((rows, width), 1) < limit, raw_ref[...].astype(F32), 0.0).astype(BF16)


def first_kernel(rhs, counts_ref, sizes_ref, kernel_ref, lower_ref, map_ref, duals_ref,
                 send_ref, inv_ref,
                 count_s, size_s, raw_ref, tri_ref, row_ref, x_ref, acc_ref, mix_ref, block_ref, sol_ref, sems, small_sems):
    modes, sub, width = kernel_ref.shape
    rows = modes * sub
    ck = lower_ref.shape[0]
    lanes = inv_ref.shape[1]
    count, _, step = x_ref.shape
    copy = slab_copies(duals_ref, x_ref, sems)
    small = [
        pltpu.make_async_copy(src, dst, small_sems.at[n])
        for n, (src, dst) in enumerate(
            (
                (lower_ref, tri_ref),
                (map_ref, row_ref),
                (counts_ref, count_s),
                (sizes_ref, size_s),
                (kernel_ref.reshape(rows, width), raw_ref),
            )
        )
    ]
    for one in small:
        one.start()
    for n in range(count):
        copy(n).start()

    place = lax.axis_index("clus").astype(jnp.int32)
    small[0].wait()
    small[1].wait()
    lower = tri_ref[...]
    eye = iota((ck, ck), 0) == iota((ck, ck), 1)
    scale = 1.0 / jnp.sum(jnp.where(eye, lower, 0.0), axis=1, keepdims=True)
    below = jnp.where(iota((ck, ck), 0) > iota((ck, ck), 1), lower * scale, 0.0)
    sol = jnp.where(iota((ck, lanes), 1) == rhs + iota((ck, lanes), 0), scale, 0.0)
    for i in range(ck - 1):
        sol = sol - below[:, i : i + 1] * sol[i : i + 1, :]
    inv_ref[...] = sol
    wanted = iota((rows, ck), 1) == place * rows + iota((rows, ck), 0)
    own_map = jnp.sum(jnp.where(wanted, row_ref[...].astype(F32), 0.0), axis=1, keepdims=True)
    for c in range(lanes // LANES):
        cols = slice(c * LANES, (c + 1) * LANES)
        sol_ref[c] = sol[:, cols]
        block_ref[:, cols] = sol_ref[c, pl.ds(place * rows, rows), :]
    block_ref[...] += jnp.where(iota((rows, lanes), 1) == rhs + ck, own_map, 0.0)

    for one in small[2:]:
        one.wait()
    masked = mask_kernel(raw_ref, count_s, size_s, sub)
    acc_ref[...] = jnp.zeros_like(acc_ref)
    total = jnp.zeros((rows, rhs * sub), F32)
    for n in range(count):
        copy(n).wait()
        total = total + dot(masked[:, n * step : (n + 1) * step], x_ref[n], NT)
    same = iota((rows, rhs * sub), 0) % sub == iota((rows, rhs * sub), 1) % sub
    acc_ref[:rows, :] = jnp.where(same, total, 0.0)
    mixed = dot_exact(acc_ref[...], rows_of_slots(sub, rhs, lanes), NN)
    for c in range(lanes // LANES):
        cols = slice(c * LANES, (c + 1) * LANES)
        mix_ref[c] = mixed[:, cols]
        for s in range(sub):
            here = slice(s * modes, (s + 1) * modes)
            block_ref[here, cols] += mix_ref[c, pl.ds(s, modes, stride=sub), :]
    group = 2 if send_ref.shape[0] % (2 * rows) == 0 else 1
    block = jnp.concatenate([block_ref[...]] * group, axis=0)
    for d in range(send_ref.shape[0] // (rows * group)):
        send_ref[pl.ds(d * rows * group, rows * group), :] = block


def middle_kernel(rhs, modes, inv_ref, picked_ref, coarse_ref, turned_ref, turn_ref):
    ck = picked_ref.shape[0]
    members = lax.axis_size("clus")
    rows = ck // members
    sub = rows // modes
    place = lax.axis_index("clus").astype(jnp.int32)
    turn_ref[...] = inv_ref[:, rhs : rhs + ck].T
    turned_ref[...] = jnp.zeros_like(turned_ref)
    for s in range(sub):
        turned_ref[pl.ds(s, modes, stride=sub), :] = turn_ref[pl.ds(place * rows + s * modes, modes), :]
    coarse_ref[...] = lax.dot_general(turned_ref[...], picked_ref[...], NN, precision=HI, preferred_element_type=F32)


def write_out(corr_of, counts_ref, sizes_ref, kernel_ref, duals_ref, out_ref,
              count_s, size_s, raw_ref, x_ref, o_ref, in_sems, out_sems, small_sems):
    modes, sub, width = kernel_ref.shape
    rows = modes * sub
    count, flat, step = x_ref.shape
    rhs = flat // sub
    in_copy = slab_copies(duals_ref, x_ref, in_sems)
    out_copy = slab_copies(out_ref, o_ref, out_sems, back=True)
    small = [
        pltpu.make_async_copy(src, dst, small_sems.at[n])
        for n, (src, dst) in enumerate(
            ((counts_ref, count_s), (sizes_ref, size_s), (kernel_ref.reshape(rows, width), raw_ref))
        )
    ]
    for one in small:
        one.start()
    for n in range(count):
        in_copy(n).start()
    corr = corr_of().astype(BF16)
    for one in small:
        one.wait()
    masked = mask_kernel(raw_ref, count_s, size_s, sub)
    wide = dot(rows_of_slots(sub, rhs, rhs), corr, NT)
    same = iota(wide.shape, 0) % sub == iota(wide.shape, 1) % sub
    wide = jnp.where(same, wide, 0.0)[:, :rows].astype(BF16)
    for n in range(count):
        in_copy(n).wait()
        delta = dot(wide, masked[:, n * step : (n + 1) * step], NN)
        o_ref[n] = (x_ref[n].astype(F32) - delta).astype(BF16)
        out_copy(n).start()
    for n in range(count):
        out_copy(n).wait()


def last_kernel(rhs, recv_ref, coarse_ref, turned_ref, counts_ref, sizes_ref, kernel_ref, duals_ref, out_ref,
                block_ref, sum_ref, *rest):
    def corr_of():
        total = recv_ref.shape[0]
        gk = coarse_ref.shape[1]
        ck = turned_ref.shape[1]
        cluster = lax.axis_index("wide").astype(jnp.int32)
        block_ref[...] = jnp.zeros_like(block_ref)
        for w in range(total // ck):
            here = slice(w * ck, (w + 1) * ck)
            block_ref[here, here] = recv_ref[here, rhs : rhs + ck]
        forward = dot_parts(block_ref[...], recv_ref[:, :rhs], NN)
        target = recv_ref[:, rhs + ck : rhs + ck + 1].astype(jnp.int32)
        hot = (target == iota((total, gk), 1)).astype(F32).astype(BF16)
        taken = dot_exact(coarse_ref[...], hot, NT)
        sum_ref[...] = forward
        mine = sum_ref[pl.ds(pl.multiple_of(cluster * ck, ck), ck), :]
        return dot_parts(turned_ref[...], mine, NN) - dot_parts(taken, forward, NN)

    write_out(corr_of, counts_ref, sizes_ref, kernel_ref, duals_ref, out_ref, *rest)


def last_kernel_plain(corr_ref, counts_ref, sizes_ref, kernel_ref, duals_ref, out_ref, *rest):
    write_out(lambda: corr_ref[...], counts_ref, sizes_ref, kernel_ref, duals_ref, out_ref, *rest)


def per_device(duals, kernel, sub_counts, dual_sizes, cluster_factor, coarse_map, coarse_inverse):
    rhs, sub, width = duals.shape
    modes = kernel.shape[1]
    rows = sub * modes
    padded = up(rows, 16)
    clusters = lax.axis_size("wide")
    members = lax.axis_size("clus")
    devices = clusters * members
    total = devices * rows
    ck = cluster_factor.shape[1]
    gk, own_cols = coarse_inverse.shape
    lanes = up(rhs + ck + 1, LANES)
    count = chunks_of(width)
    step = width // count
    place = lax.axis_index("clus").astype(jnp.int32)
    counts = sub_counts.reshape(1, 1)
    sizes = stay(dual_sizes)
    modes_first = stay(kernel.transpose(1, 0, 2))
    vectors = stay(duals)
    slabs = (count, rhs * sub, step)

    send, inv = pl.pallas_call(
        functools.partial(first_kernel, rhs),
        out_shape=(jax.ShapeDtypeStruct((total, lanes), F32), jax.ShapeDtypeStruct((ck, lanes), F32)),
        in_specs=[HBM] * 6,
        out_specs=(VMEM, VMEM),
        scratch_shapes=[
            pltpu.SMEM((1, 1), jnp.int32),
            pltpu.SMEM((sub,), jnp.int32),
            pltpu.VMEM((rows, width), BF16),
            pltpu.VMEM((ck, ck), F32),
            pltpu.VMEM((1, ck), jnp.int32),
            pltpu.VMEM(slabs, BF16),
            pltpu.VMEM((padded, rhs * sub), F32),
            pltpu.VMEM((lanes // LANES, padded, LANES), F32),
            pltpu.VMEM((rows, lanes), F32),
            pltpu.VMEM((lanes // LANES, ck, LANES), F32),
            pltpu.SemaphoreType.DMA((count,)),
            pltpu.SemaphoreType.DMA((5,)),
        ],
        compiler_params=pltpu.CompilerParams(vmem_limit_bytes=FIRST_LIMIT),
    )(counts, sizes, modes_first, stay(cluster_factor[0]), stay(coarse_map), vectors)

    spread = send.reshape(devices, rows, lanes // LANES, LANES)
    recv = lax.all_to_all(spread, ("wide", "clus"), 0, 0)

    inv, rows_map, coarse_t, _ = lax.optimization_barrier((inv, coarse_map[0], coarse_inverse.T, send))
    hot = (rows_map[:, None] == place * own_cols + iota((ck, own_cols), 1)).astype(F32)
    part = jnp.dot(hot, coarse_t, precision=HI)
    picked = part
    for shift in range(1, members):
        picked = picked + lax.ppermute(part, "clus", [(i, (i + shift) % members) for i in range(members)])
    params = pltpu.CompilerParams(vmem_limit_bytes=LAST_LIMIT)
    coarse, turned = pl.pallas_call(
        functools.partial(middle_kernel, rhs, modes),
        out_shape=(jax.ShapeDtypeStruct((padded, gk), F32), jax.ShapeDtypeStruct((padded, ck), F32)),
        in_specs=[VMEM, VMEM],
        out_specs=(VMEM, VMEM),
        scratch_shapes=[pltpu.VMEM((ck, ck), F32)],
        compiler_params=params,
    )(inv, picked)

    out_shape = jax.ShapeDtypeStruct(duals.shape, BF16)
    scratch = [
        pltpu.SMEM((1, 1), jnp.int32),
        pltpu.SMEM((sub,), jnp.int32),
        pltpu.VMEM((rows, width), BF16),
        pltpu.VMEM(slabs, BF16),
        pltpu.VMEM(slabs, BF16),
        pltpu.SemaphoreType.DMA((count,)),
        pltpu.SemaphoreType.DMA((count,)),
        pltpu.SemaphoreType.DMA((3,)),
    ]
    if total * max(total, gk) <= 2**20:
        return pl.pallas_call(
            functools.partial(last_kernel, rhs),
            out_shape=out_shape,
            in_specs=[VMEM] * 3 + [HBM] * 4,
            out_specs=HBM,
            scratch_shapes=[pltpu.VMEM((total, total), F32), pltpu.VMEM((total, rhs), F32), *scratch],
            compiler_params=params,
        )(recv.reshape(total, lanes), coarse, turned, counts, sizes, modes_first, vectors)

    blocks = recv.reshape(clusters, ck, lanes)
    forward = jnp.einsum("wam,wmr->war", blocks[:, :, rhs : rhs + ck], blocks[:, :, :rhs], precision=HI)
    target = blocks[:, :, rhs + ck].astype(jnp.int32).reshape(total)
    all_hot = (target[:, None] == iota((total, gk), 1)).astype(F32)
    gsum = lax.dot_general(all_hot, forward.reshape(total, rhs), (((0,), (0,)), ((), ())), precision=HI)
    mine = lax.dynamic_index_in_dim(forward, lax.axis_index("wide"), 0, keepdims=False)
    corr = jnp.dot(turned, mine, precision=HI) - jnp.dot(coarse, gsum, precision=HI)
    return pl.pallas_call(
        last_kernel_plain,
        out_shape=out_shape,
        in_specs=[VMEM] + [HBM] * 4,
        out_specs=HBM,
        scratch_shapes=scratch,
        compiler_params=params,
    )(corr, counts, sizes, modes_first, vectors)


def solution(mesh):
    in_specs = (
        P(None, ("wide", "clus"), None),
        P(("wide", "clus"), None, None),
        P(("wide", "clus")),
        P(("wide", "clus")),
        P("wide", None, None),
        P("wide", None),
        P(None, "clus"),
    )
    out_specs = P(None, ("wide", "clus"), None)
    return jax.shard_map(
        per_device, mesh=mesh, in_specs=in_specs, out_specs=out_specs, check_vma=False
    )
```

```python
import functools

import jax
import jax.numpy as jnp
from jax import lax
from jax.experimental import pallas as pl
from jax.experimental.pallas import tpu as pltpu
from jax.sharding import PartitionSpec as P

F32 = jnp.float32
BF16 = jnp.bfloat16
LANES = 128
HI = lax.Precision.HIGHEST
NT = (((1,), (1,)), ((), ()))
NN = (((1,), (0,)), ((), ()))
VMEM = pl.BlockSpec(memory_space=pltpu.VMEM)
HBM = pl.BlockSpec(memory_space=pltpu.HBM)
FIRST_LIMIT = 60 * 2**20
LAST_LIMIT = 20 * 2**20


def iota(shape, dim):
    return lax.broadcasted_iota(jnp.int32, shape, dim)


def stay(x):
    return pltpu.with_memory_space_constraint(x, pltpu.HBM)


def up(value, step):
    return -(-value // step) * step


def split(x, parts):
    out = []
    for n in range(parts):
        head = x.astype(BF16)
        out.append(head)
        if n + 1 < parts:
            x = x - head.astype(F32)
    return out


def dot(a, b, dims):
    return lax.dot_general(a, b, dims, preferred_element_type=F32)


def dot_parts(a, b, dims):
    a_hi, a_lo = split(a, 2)
    b_hi, b_lo = split(b, 2)
    rows = a.shape[0]
    both = dot(jnp.concatenate([a_hi, a_lo], axis=0), b_hi, dims)
    return both[:rows] + both[rows:] + dot(a_hi, b_lo, dims)


def dot_exact(a, hot, dims):
    rows = a.shape[0]
    parts = dot(jnp.concatenate(split(a, 3), axis=0), hot, dims)
    return parts[:rows] + parts[rows : 2 * rows] + parts[2 * rows :]


def chunks_of(width):
    for count in (5, 3, 2):
        if width % (count * LANES) == 0:
            return count
    return 1


def rows_of_slots(sub, rhs, lanes):
    return (iota((rhs * sub, lanes), 0) // sub == iota((rhs * sub, lanes), 1)).astype(F32).astype(BF16)


def slab_copies(whole_ref, slabs_ref, sems, back=False):
    count, rows, step = slabs_ref.shape
    flat = whole_ref.reshape(rows, count * step)

    def copy(n):
        part = flat.at[:, pl.ds(n * step, step)]
        ends = (slabs_ref.at[n], part) if back else (part, slabs_ref.at[n])
        return pltpu.make_async_copy(*ends, sems.at[n])

    return copy


def mask_kernel(raw_ref, count_s, size_s, sub):
    rows, width = raw_ref.shape
    slot = iota((rows, width), 0) % sub
    limit = jnp.zeros((rows, width), jnp.int32)
    for s in range(sub):
        size = jnp.where(s < count_s[0, 0], size_s[s], 0)
        limit = jnp.where(slot == s, size, limit)
    return jnp.where(iota((rows, width), 1) < limit, raw_ref[...].astype(F32), 0.0).astype(BF16)


def first_kernel(rhs, counts_ref, sizes_ref, kernel_ref, lower_ref, map_ref, duals_ref,
                 send_ref, inv_ref,
                 count_s, size_s, raw_ref, tri_ref, row_ref, x_ref, acc_ref, mix_ref, block_ref, sol_ref, sems, small_sems):
    modes, sub, width = kernel_ref.shape
    rows = modes * sub
    ck = lower_ref.shape[0]
    lanes = inv_ref.shape[1]
    count, _, step = x_ref.shape
    copy = slab_copies(duals_ref, x_ref, sems)
    small = [
        pltpu.make_async_copy(src, dst, small_sems.at[n])
        for n, (src, dst) in enumerate(
            (
                (lower_ref, tri_ref),
                (map_ref, row_ref),
                (counts_ref, count_s),
                (sizes_ref, size_s),
                (kernel_ref.reshape(rows, width), raw_ref),
            )
        )
    ]
    for one in small:
        one.start()
    for n in range(count):
        copy(n).start()

    place = lax.axis_index("clus").astype(jnp.int32)
    small[0].wait()
    small[1].wait()
    lower = tri_ref[...]
    eye = iota((ck, ck), 0) == iota((ck, ck), 1)
    scale = 1.0 / jnp.sum(jnp.where(eye, lower, 0.0), axis=1, keepdims=True)
    below = jnp.where(iota((ck, ck), 0) > iota((ck, ck), 1), lower * scale, 0.0)
    sol = jnp.where(iota((ck, lanes), 1) == rhs + iota((ck, lanes), 0), scale, 0.0)
    for i in range(ck - 1):
        sol = sol - below[:, i : i + 1] * sol[i : i + 1, :]
    inv_ref[...] = sol
    wanted = iota((rows, ck), 1) == place * rows + iota((rows, ck), 0)
    own_map = jnp.sum(jnp.where(wanted, row_ref[...].astype(F32), 0.0), axis=1, keepdims=True)
    for c in range(lanes // LANES):
        cols = slice(c * LANES, (c + 1) * LANES)
        sol_ref[c] = sol[:, cols]
        block_ref[:, cols] = sol_ref[c, pl.ds(place * rows, rows), :]
    block_ref[...] += jnp.where(iota((rows, lanes), 1) == rhs + ck, own_map, 0.0)

    for one in small[2:]:
        one.wait()
    masked = mask_kernel(raw_ref, count_s, size_s, sub)
    acc_ref[...] = jnp.zeros_like(acc_ref)
    total = jnp.zeros((rows, rhs * sub), F32)
    for n in range(count):
        copy(n).wait()
        total = total + dot(masked[:, n * step : (n + 1) * step], x_ref[n], NT)
    same = iota((rows, rhs * sub), 0) % sub == iota((rows, rhs * sub), 1) % sub
    acc_ref[:rows, :] = jnp.where(same, total, 0.0)
    mixed = dot_exact(acc_ref[...], rows_of_slots(sub, rhs, lanes), NN)
    for c in range(lanes // LANES):
        cols = slice(c * LANES, (c + 1) * LANES)
        mix_ref[c] = mixed[:, cols]
        for s in range(sub):
            here = slice(s * modes, (s + 1) * modes)
            block_ref[here, cols] += mix_ref[c, pl.ds(s, modes, stride=sub), :]
    group = 2 if send_ref.shape[0] % (2 * rows) == 0 else 1
    block = jnp.concatenate([block_ref[...]] * group, axis=0)
    for d in range(send_ref.shape[0] // (rows * group)):
        send_ref[pl.ds(d * rows * group, rows * group), :] = block


def middle_kernel(rhs, inv_ref, picked_ref, counts_ref, sizes_ref, kernel_ref, duals_ref,
                  coarse_ref, turned_ref, masked_ref, x_ref,
                  count_s, size_s, raw_ref, turn_ref, sems, small_sems):
    modes, sub, width = kernel_ref.shape
    rows = modes * sub
    ck = picked_ref.shape[0]
    count = x_ref.shape[0]
    copy = slab_copies(duals_ref, x_ref, sems)
    small = [
        pltpu.make_async_copy(src, dst, small_sems.at[n])
        for n, (src, dst) in enumerate(
            ((counts_ref, count_s), (sizes_ref, size_s), (kernel_ref.reshape(rows, width), raw_ref))
        )
    ]
    for one in small:
        one.start()
    for n in range(count):
        copy(n).start()
    place = lax.axis_index("clus").astype(jnp.int32)
    turn_ref[...] = inv_ref[:, rhs : rhs + ck].T
    turned_ref[...] = jnp.zeros_like(turned_ref)
    for s in range(sub):
        turned_ref[pl.ds(s, modes, stride=sub), :] = turn_ref[pl.ds(place * rows + s * modes, modes), :]
    coarse_ref[...] = lax.dot_general(turned_ref[...], picked_ref[...], NN, precision=HI, preferred_element_type=F32)
    for one in small:
        one.wait()
    masked_ref[...] = mask_kernel(raw_ref, count_s, size_s, sub)
    for n in range(count):
        copy(n).wait()


def write_out(corr, sub, masked_ref, x_ref, out_ref, o_ref, sems):
    rows = masked_ref.shape[0]
    count, flat, step = x_ref.shape
    rhs = flat // sub
    copy = slab_copies(out_ref, o_ref, sems, back=True)
    wide = dot(rows_of_slots(sub, rhs, rhs), corr, NT)
    same = iota(wide.shape, 0) % sub == iota(wide.shape, 1) % sub
    wide = jnp.where(same, wide, 0.0)[:, :rows].astype(BF16)
    for n in range(count):
        delta = dot(wide, masked_ref[:, n * step : (n + 1) * step], NN)
        o_ref[n] = (x_ref[n].astype(F32) - delta).astype(BF16)
        copy(n).start()
    for n in range(count):
        copy(n).wait()


def last_kernel(rhs, sub, recv_ref, coarse_ref, turned_ref, masked_ref, x_ref, out_ref, block_ref, sum_ref, o_ref, sems):
    total = recv_ref.shape[0]
    gk = coarse_ref.shape[1]
    ck = turned_ref.shape[1]
    cluster = lax.axis_index("wide").astype(jnp.int32)
    block_ref[...] = jnp.zeros_like(block_ref)
    for w in range(total // ck):
        here = slice(w * ck, (w + 1) * ck)
        block_ref[here, here] = recv_ref[here, rhs : rhs + ck]
    forward = dot_parts(block_ref[...], recv_ref[:, :rhs], NN)
    target = recv_ref[:, rhs + ck : rhs + ck + 1].astype(jnp.int32)
    hot = (target == iota((total, gk), 1)).astype(F32).astype(BF16)
    taken = dot_exact(coarse_ref[...], hot, NT)
    sum_ref[...] = forward
    mine = sum_ref[pl.ds(pl.multiple_of(cluster * ck, ck), ck), :]
    corr = dot_parts(turned_ref[...], mine, NN) - dot_parts(taken, forward, NN)
    write_out(corr.astype(BF16), sub, masked_ref, x_ref, out_ref, o_ref, sems)


def last_kernel_plain(sub, corr_ref, masked_ref, x_ref, out_ref, o_ref, sems):
    write_out(corr_ref[...].astype(BF16), sub, masked_ref, x_ref, out_ref, o_ref, sems)


def per_device(duals, kernel, sub_counts, dual_sizes, cluster_factor, coarse_map, coarse_inverse):
    rhs, sub, width = duals.shape
    modes = kernel.shape[1]
    rows = sub * modes
    padded = up(rows, 16)
    clusters = lax.axis_size("wide")
    members = lax.axis_size("clus")
    devices = clusters * members
    total = devices * rows
    ck = cluster_factor.shape[1]
    gk, own_cols = coarse_inverse.shape
    lanes = up(rhs + ck + 1, LANES)
    count = chunks_of(width)
    step = width // count
    place = lax.axis_index("clus").astype(jnp.int32)
    counts = sub_counts.reshape(1, 1)
    sizes = stay(dual_sizes)
    modes_first = stay(kernel.transpose(1, 0, 2))
    vectors = stay(duals)
    slabs = (count, rhs * sub, step)
    small_enough = total * max(total, gk) <= 2**20
    OUT = pltpu.VMEM if small_enough else jax.ShapeDtypeStruct

    send, inv = pl.pallas_call(
        functools.partial(first_kernel, rhs),
        out_shape=(jax.ShapeDtypeStruct((total, lanes), F32), OUT((ck, lanes), F32)),
        in_specs=[HBM] * 6,
        out_specs=(VMEM, VMEM),
        scratch_shapes=[
            pltpu.SMEM((1, 1), jnp.int32),
            pltpu.SMEM((sub,), jnp.int32),
            pltpu.VMEM((rows, width), BF16),
            pltpu.VMEM((ck, ck), F32),
            pltpu.VMEM((1, ck), jnp.int32),
            pltpu.VMEM(slabs, BF16),
            pltpu.VMEM((padded, rhs * sub), F32),
            pltpu.VMEM((lanes // LANES, padded, LANES), F32),
            pltpu.VMEM((rows, lanes), F32),
            pltpu.VMEM((lanes // LANES, ck, LANES), F32),
            pltpu.SemaphoreType.DMA((count,)),
            pltpu.SemaphoreType.DMA((5,)),
        ],
        compiler_params=pltpu.CompilerParams(vmem_limit_bytes=FIRST_LIMIT),
    )(counts, sizes, modes_first, stay(cluster_factor[0]), stay(coarse_map), vectors)

    spread = send.reshape(devices, rows, lanes // LANES, LANES)
    recv = lax.all_to_all(spread, ("wide", "clus"), 0, 0)

    inv, rows_map, coarse_t, _ = lax.optimization_barrier((inv, coarse_map[0], coarse_inverse.T, send))
    hot = (rows_map[:, None] == place * own_cols + iota((ck, own_cols), 1)).astype(F32)
    part = jnp.dot(hot, coarse_t, precision=HI)
    picked = part
    for shift in range(1, members):
        picked = picked + lax.ppermute(part, "clus", [(i, (i + shift) % members) for i in range(members)])
    params = pltpu.CompilerParams(vmem_limit_bytes=LAST_LIMIT)
    coarse, turned, masked, x = pl.pallas_call(
        functools.partial(middle_kernel, rhs),
        out_shape=(
            OUT((padded, gk), F32),
            OUT((padded, ck), F32),
            OUT((rows, width), BF16),
            OUT(slabs, BF16),
        ),
        in_specs=[VMEM, VMEM] + [HBM] * 4,
        out_specs=(VMEM,) * 4,
        scratch_shapes=[
            pltpu.SMEM((1, 1), jnp.int32),
            pltpu.SMEM((sub,), jnp.int32),
            pltpu.VMEM((rows, width), BF16),
            pltpu.VMEM((ck, ck), F32),
            pltpu.SemaphoreType.DMA((count,)),
            pltpu.SemaphoreType.DMA((3,)),
        ],
        compiler_params=params,
    )(inv, picked, counts, sizes, modes_first, vectors)

    out_shape = jax.ShapeDtypeStruct(duals.shape, BF16)
    scratch = [pltpu.VMEM(slabs, BF16), pltpu.SemaphoreType.DMA((count,))]
    if small_enough:
        return pl.pallas_call(
            functools.partial(last_kernel, rhs, sub),
            out_shape=out_shape,
            in_specs=[VMEM] * 5,
            out_specs=HBM,
            scratch_shapes=[pltpu.VMEM((total, total), F32), pltpu.VMEM((total, rhs), F32), *scratch],
            compiler_params=params,
        )(recv.reshape(total, lanes), coarse, turned, masked, x)

    blocks = recv.reshape(clusters, ck, lanes)
    forward = jnp.einsum("wam,wmr->war", blocks[:, :, rhs : rhs + ck], blocks[:, :, :rhs], precision=HI)
    target = blocks[:, :, rhs + ck].astype(jnp.int32).reshape(total)
    all_hot = (target[:, None] == iota((total, gk), 1)).astype(F32)
    gsum = lax.dot_general(all_hot, forward.reshape(total, rhs), (((0,), (0,)), ((), ())), precision=HI)
    mine = lax.dynamic_index_in_dim(forward, lax.axis_index("wide"), 0, keepdims=False)
    corr = jnp.dot(turned, mine, precision=HI) - jnp.dot(coarse, gsum, precision=HI)
    return pl.pallas_call(
        functools.partial(last_kernel_plain, sub),
        out_shape=out_shape,
        in_specs=[VMEM] * 3,
        out_specs=HBM,
        scratch_shapes=scratch,
        compiler_params=params,
    )(corr, masked, x)


def solution(mesh):
    in_specs = (
        P(None, ("wide", "clus"), None),
        P(("wide", "clus"), None, None),
        P(("wide", "clus")),
        P(("wide", "clus")),
        P("wide", None, None),
        P("wide", None),
        P(None, "clus"),
    )
    out_specs = P(None, ("wide", "clus"), None)
    return jax.shard_map(
        per_device, mesh=mesh, in_specs=in_specs, out_specs=out_specs, check_vma=False
    )
```

```python
import functools

import jax
import jax.numpy as jnp
from jax import lax
from jax.experimental import pallas as pl
from jax.experimental.pallas import tpu as pltpu
from jax.sharding import PartitionSpec as P

F32 = jnp.float32
BF16 = jnp.bfloat16
LANES = 128
HI = lax.Precision.HIGHEST
NT = (((1,), (1,)), ((), ()))
NN = (((1,), (0,)), ((), ()))
VMEM = pl.BlockSpec(memory_space=pltpu.VMEM)
HBM = pl.BlockSpec(memory_space=pltpu.HBM)
FIRST_LIMIT = 60 * 2**20
LAST_LIMIT = 20 * 2**20
AHEAD = 3


def iota(shape, dim):
    return lax.broadcasted_iota(jnp.int32, shape, dim)


def stay(x):
    return pltpu.with_memory_space_constraint(x, pltpu.HBM)


def up(value, step):
    return -(-value // step) * step


def split(x, parts):
    out = []
    for n in range(parts):
        head = x.astype(BF16)
        out.append(head)
        if n + 1 < parts:
            x = x - head.astype(F32)
    return out


def dot(a, b, dims):
    return lax.dot_general(a, b, dims, preferred_element_type=F32)


def dot_parts(a, b, dims):
    a_hi, a_lo = split(a, 2)
    b_hi, b_lo = split(b, 2)
    rows = a.shape[0]
    both = dot(jnp.concatenate([a_hi, a_lo], axis=0), b_hi, dims)
    return both[:rows] + both[rows:] + dot(a_hi, b_lo, dims)


def dot_exact(a, hot, dims):
    rows = a.shape[0]
    parts = dot(jnp.concatenate(split(a, 3), axis=0), hot, dims)
    return parts[:rows] + parts[rows : 2 * rows] + parts[2 * rows :]


def chunks_of(width):
    for count in (5, 3, 2):
        if width % (count * LANES) == 0:
            return count
    return 1


def rows_of_slots(sub, rhs, lanes):
    return (iota((rhs * sub, lanes), 0) // sub == iota((rhs * sub, lanes), 1)).astype(F32).astype(BF16)


def slab_copies(whole_ref, slabs_ref, sems, back=False):
    count, _, step = slabs_ref.shape
    rows = whole_ref.shape[0] * whole_ref.shape[1]
    flat = whole_ref.reshape(rows, count * step)

    def copy(n):
        part = flat.at[:, pl.ds(n * step, step)]
        slab = slabs_ref.at[n, pl.ds(0, rows)]
        ends = (slab, part) if back else (part, slab)
        return pltpu.make_async_copy(*ends, sems.at[n])

    return copy


def mask_kernel(raw_ref, count_s, size_s, sub):
    rows, width = raw_ref.shape
    slot = iota((rows, width), 0) % sub
    limit = jnp.zeros((rows, width), jnp.int32)
    for s in range(sub):
        size = jnp.where(s < count_s[0, 0], size_s[s], 0)
        limit = jnp.where(slot == s, size, limit)
    return jnp.where(iota((rows, width), 1) < limit, raw_ref[...].astype(F32), 0.0).astype(BF16)


def first_kernel(rhs, counts_ref, sizes_ref, kernel_ref, lower_ref, map_ref, duals_ref,
                 send_ref, inv_ref,
                 count_s, size_s, raw_ref, tri_ref, row_ref, x_ref, acc_ref, mix_ref, block_ref, sol_ref, sems, small_sems):
    modes, sub, width = kernel_ref.shape
    rows = modes * sub
    ck = lower_ref.shape[0]
    lanes = inv_ref.shape[1]
    count, _, step = x_ref.shape
    copy = slab_copies(duals_ref, x_ref, sems)
    small = [
        pltpu.make_async_copy(src, dst, small_sems.at[n])
        for n, (src, dst) in enumerate(
            (
                (lower_ref, tri_ref),
                (map_ref, row_ref),
                (counts_ref, count_s),
                (sizes_ref, size_s),
                (kernel_ref.reshape(rows, width), raw_ref),
            )
        )
    ]
    for one in small:
        one.start()
    for n in range(count):
        copy(n).start()

    place = lax.axis_index("clus").astype(jnp.int32)
    small[0].wait()
    small[1].wait()
    lower = tri_ref[...]
    eye = iota((ck, ck), 0) == iota((ck, ck), 1)
    scale = 1.0 / jnp.sum(jnp.where(eye, lower, 0.0), axis=1, keepdims=True)
    below = jnp.where(iota((ck, ck), 0) > iota((ck, ck), 1), lower * scale, 0.0)
    sol = jnp.where(iota((ck, lanes), 1) == rhs + iota((ck, lanes), 0), scale, 0.0)
    for i in range(ck - 1):
        sol = sol - below[:, i : i + 1] * sol[i : i + 1, :]
    inv_ref[...] = sol
    wanted = iota((rows, ck), 1) == place * rows + iota((rows, ck), 0)
    own_map = jnp.sum(jnp.where(wanted, row_ref[...].astype(F32), 0.0), axis=1, keepdims=True)
    for c in range(lanes // LANES):
        cols = slice(c * LANES, (c + 1) * LANES)
        sol_ref[c] = sol[:, cols]
        block_ref[:, cols] = sol_ref[c, pl.ds(place * rows, rows), :]
    block_ref[...] += jnp.where(iota((rows, lanes), 1) == rhs + ck, own_map, 0.0)

    for one in small[2:]:
        one.wait()
    masked = mask_kernel(raw_ref, count_s, size_s, sub)
    acc_ref[...] = jnp.zeros_like(acc_ref)
    total = jnp.zeros((rows, rhs * sub), F32)
    for n in range(count):
        copy(n).wait()
        total = total + dot(masked[:, n * step : (n + 1) * step], x_ref[n], NT)
    same = iota((rows, rhs * sub), 0) % sub == iota((rows, rhs * sub), 1) % sub
    acc_ref[:rows, :] = jnp.where(same, total, 0.0)
    mixed = dot_exact(acc_ref[...], rows_of_slots(sub, rhs, lanes), NN)
    for c in range(lanes // LANES):
        cols = slice(c * LANES, (c + 1) * LANES)
        mix_ref[c] = mixed[:, cols]
        for s in range(sub):
            here = slice(s * modes, (s + 1) * modes)
            block_ref[here, cols] += mix_ref[c, pl.ds(s, modes, stride=sub), :]
    group = 2 if send_ref.shape[0] % (2 * rows) == 0 else 1
    block = jnp.concatenate([block_ref[...]] * group, axis=0)
    for d in range(send_ref.shape[0] // (rows * group)):
        send_ref[pl.ds(d * rows * group, rows * group), :] = block


def middle_kernel(rhs, inv_ref, picked_ref, counts_ref, sizes_ref, kernel_ref, duals_ref,
                  coarse_ref, turned_ref, x_ref,
                  count_s, size_s, raw_ref, turn_ref, sems, small_sems):
    modes, sub, width = kernel_ref.shape
    rows = modes * sub
    ck = picked_ref.shape[0]
    count, deep, step = x_ref.shape
    flat = duals_ref.shape[0] * sub
    copy = slab_copies(duals_ref, x_ref, sems)
    small = [
        pltpu.make_async_copy(src, dst, small_sems.at[n])
        for n, (src, dst) in enumerate(
            ((counts_ref, count_s), (sizes_ref, size_s), (kernel_ref.reshape(rows, width), raw_ref))
        )
    ]
    for one in small:
        one.start()
    for n in range(count):
        copy(n).start()
    place = lax.axis_index("clus").astype(jnp.int32)
    turn_ref[...] = inv_ref[:, rhs : rhs + ck].T
    turned_ref[...] = jnp.zeros_like(turned_ref)
    for s in range(sub):
        turned_ref[pl.ds(s, modes, stride=sub), :] = turn_ref[pl.ds(place * rows + s * modes, modes), :]
    coarse_ref[...] = lax.dot_general(turned_ref[...], picked_ref[...], NN, precision=HI, preferred_element_type=F32)
    for one in small:
        one.wait()
    masked = mask_kernel(raw_ref, count_s, size_s, sub)
    for n in range(count):
        x_ref[n, flat:, :] = jnp.zeros((deep - flat, step), BF16)
        x_ref[n, flat : flat + rows, :] = masked[:, n * step : (n + 1) * step]
    for n in range(count):
        copy(n).wait()


def write_out(corr, sub, x_ref, out_ref, corr_ref, o_ref, sems):
    flat, rhs = o_ref.shape[1], corr_ref.shape[1]
    count, deep, step = x_ref.shape
    copy = slab_copies(out_ref, o_ref, sems, back=True)
    corr_ref[:flat, :] = jnp.zeros((flat, rhs), BF16)
    corr_ref[flat:, :] = -corr
    wide = dot(rows_of_slots(sub, rhs, rhs), corr_ref[...], NT)
    row, col = iota(wide.shape, 0), iota(wide.shape, 1)
    same = (col >= flat) & (row % sub == col % sub)
    left = jnp.where(same, wide, (row == col).astype(F32)).astype(BF16)
    tile = 2 * LANES if step % (2 * LANES) == 0 else LANES
    tiles = [(n, slice(c, c + tile)) for n in range(count) for c in range(0, step, tile)]
    waiting = []
    for n, cols in [*tiles, *[(None, None)] * AHEAD]:
        if n is not None:
            waiting.append((n, cols, dot(left, x_ref[n, :, cols], NN)))
        if len(waiting) > AHEAD or n is None and waiting:
            done, where, value = waiting.pop(0)
            o_ref[done, :, where] = value.astype(BF16)
            if where.stop == step:
                copy(done).start()
    for n in range(count):
        copy(n).wait()


def block_product(recv_ref, rhs, ck, block_ref):
    total = recv_ref.shape[0]
    block_ref[...] = jnp.zeros_like(block_ref)
    for w in range(total // ck):
        here = slice(w * ck, (w + 1) * ck)
        block_ref[here, here] = recv_ref[here, rhs : rhs + ck]
    spans = []
    for start in range(0, total, LANES):
        stop = min(start + LANES, total)
        low = start // ck * ck // 16 * 16
        high = min(up(up(stop, ck), 16), total)
        spans.append((low, high, dot_parts(block_ref[low:high, start:stop], recv_ref[start:stop, :rhs], NN)))
    return spans


def last_kernel(rhs, sub, recv_ref, coarse_ref, turned_ref, x_ref, out_ref, block_ref, sum_ref, corr_ref, o_ref, sems):
    total = recv_ref.shape[0]
    gk = coarse_ref.shape[1]
    ck = turned_ref.shape[1]
    cluster = lax.axis_index("wide").astype(jnp.int32)
    done = 0
    for low, high, part in block_product(recv_ref, rhs, ck, block_ref):
        if low < done:
            sum_ref[low:done, :] += part[: done - low]
        sum_ref[done:high, :] = part[done - low :]
        done = high
    target = recv_ref[:, rhs + ck : rhs + ck + 1].astype(jnp.int32)
    hot = (target == iota((total, gk), 1)).astype(F32).astype(BF16)
    taken = dot_exact(coarse_ref[...], hot, NT)
    mine = sum_ref[pl.ds(pl.multiple_of(cluster * ck, ck), ck), :]
    corr = dot_parts(turned_ref[...], mine, NN) - dot_parts(taken, sum_ref[...], NN)
    write_out(corr.astype(BF16), sub, x_ref, out_ref, corr_ref, o_ref, sems)


def last_kernel_plain(sub, given_ref, x_ref, out_ref, corr_ref, o_ref, sems):
    write_out(given_ref[...].astype(BF16), sub, x_ref, out_ref, corr_ref, o_ref, sems)


def per_device(duals, kernel, sub_counts, dual_sizes, cluster_factor, coarse_map, coarse_inverse):
    rhs, sub, width = duals.shape
    modes = kernel.shape[1]
    rows = sub * modes
    padded = up(rows, 16)
    clusters = lax.axis_size("wide")
    members = lax.axis_size("clus")
    devices = clusters * members
    total = devices * rows
    ck = cluster_factor.shape[1]
    gk, own_cols = coarse_inverse.shape
    lanes = up(rhs + ck + 1, LANES)
    count = chunks_of(width)
    step = width // count
    place = lax.axis_index("clus").astype(jnp.int32)
    counts = sub_counts.reshape(1, 1)
    sizes = stay(dual_sizes)
    modes_first = stay(kernel.transpose(1, 0, 2))
    vectors = stay(duals)
    slabs = (count, rhs * sub, step)
    deeper = (count, rhs * sub + padded, step)
    small_enough = total * max(total, gk) <= 2**20
    OUT = pltpu.VMEM if small_enough else jax.ShapeDtypeStruct

    send, inv = pl.pallas_call(
        functools.partial(first_kernel, rhs),
        out_shape=(jax.ShapeDtypeStruct((total, lanes), F32), OUT((ck, lanes), F32)),
        in_specs=[HBM] * 6,
        out_specs=(VMEM, VMEM),
        scratch_shapes=[
            pltpu.SMEM((1, 1), jnp.int32),
            pltpu.SMEM((sub,), jnp.int32),
            pltpu.VMEM((rows, width), BF16),
            pltpu.VMEM((ck, ck), F32),
            pltpu.VMEM((1, ck), jnp.int32),
            pltpu.VMEM(slabs, BF16),
            pltpu.VMEM((padded, rhs * sub), F32),
            pltpu.VMEM((lanes // LANES, padded, LANES), F32),
            pltpu.VMEM((rows, lanes), F32),
            pltpu.VMEM((lanes // LANES, ck, LANES), F32),
            pltpu.SemaphoreType.DMA((count,)),
            pltpu.SemaphoreType.DMA((5,)),
        ],
        compiler_params=pltpu.CompilerParams(vmem_limit_bytes=FIRST_LIMIT),
    )(counts, sizes, modes_first, stay(cluster_factor[0]), stay(coarse_map), vectors)

    spread = send.reshape(devices, rows, lanes // LANES, LANES)
    recv = lax.all_to_all(spread, ("wide", "clus"), 0, 0)

    inv, rows_map, coarse_t, _ = lax.optimization_barrier((inv, coarse_map[0], coarse_inverse.T, send))
    hot = (rows_map[:, None] == place * own_cols + iota((ck, own_cols), 1)).astype(F32)
    part = jnp.dot(hot, coarse_t, precision=HI)
    picked = part
    for shift in range(1, members):
        picked = picked + lax.ppermute(part, "clus", [(i, (i + shift) % members) for i in range(members)])
    params = pltpu.CompilerParams(vmem_limit_bytes=LAST_LIMIT)
    coarse, turned, x = pl.pallas_call(
        functools.partial(middle_kernel, rhs),
        out_shape=(
            OUT((padded, gk), F32),
            OUT((padded, ck), F32),
            OUT(deeper, BF16),
        ),
        in_specs=[VMEM, VMEM] + [HBM] * 4,
        out_specs=(VMEM,) * 3,
        scratch_shapes=[
            pltpu.SMEM((1, 1), jnp.int32),
            pltpu.SMEM((sub,), jnp.int32),
            pltpu.VMEM((rows, width), BF16),
            pltpu.VMEM((ck, ck), F32),
            pltpu.SemaphoreType.DMA((count,)),
            pltpu.SemaphoreType.DMA((3,)),
        ],
        compiler_params=params,
    )(inv, picked, counts, sizes, modes_first, vectors)

    out_shape = jax.ShapeDtypeStruct(duals.shape, BF16)
    scratch = [
        pltpu.VMEM((rhs * sub + padded, rhs), BF16),
        pltpu.VMEM(slabs, BF16),
        pltpu.SemaphoreType.DMA((count,)),
    ]
    if small_enough:
        return pl.pallas_call(
            functools.partial(last_kernel, rhs, sub),
            out_shape=out_shape,
            in_specs=[VMEM] * 4,
            out_specs=HBM,
            scratch_shapes=[pltpu.VMEM((total, total), F32), pltpu.VMEM((total, rhs), F32), *scratch],
            compiler_params=params,
        )(recv.reshape(total, lanes), coarse, turned, x)

    blocks = recv.reshape(clusters, ck, lanes)
    forward = jnp.einsum("wam,wmr->war", blocks[:, :, rhs : rhs + ck], blocks[:, :, :rhs], precision=HI)
    target = blocks[:, :, rhs + ck].astype(jnp.int32).reshape(total)
    all_hot = (target[:, None] == iota((total, gk), 1)).astype(F32)
    gsum = lax.dot_general(all_hot, forward.reshape(total, rhs), (((0,), (0,)), ((), ())), precision=HI)
    mine = lax.dynamic_index_in_dim(forward, lax.axis_index("wide"), 0, keepdims=False)
    corr = jnp.dot(turned, mine, precision=HI) - jnp.dot(coarse, gsum, precision=HI)
    return pl.pallas_call(
        functools.partial(last_kernel_plain, sub),
        out_shape=out_shape,
        in_specs=[VMEM] * 2,
        out_specs=HBM,
        scratch_shapes=scratch,
        compiler_params=params,
    )(corr, x)


def solution(mesh):
    in_specs = (
        P(None, ("wide", "clus"), None),
        P(("wide", "clus"), None, None),
        P(("wide", "clus")),
        P(("wide", "clus")),
        P("wide", None, None),
        P("wide", None),
        P(None, "clus"),
    )
    out_specs = P(None, ("wide", "clus"), None)
    return jax.shard_map(
        per_device, mesh=mesh, in_specs=in_specs, out_specs=out_specs, check_vma=False
    )
```

```python
import functools

import jax
import jax.numpy as jnp
from jax import lax
from jax.experimental import pallas as pl
from jax.experimental.pallas import tpu as pltpu
from jax.sharding import PartitionSpec as P

F32 = jnp.float32
BF16 = jnp.bfloat16
LANES = 128
HI = lax.Precision.HIGHEST
NT = (((1,), (1,)), ((), ()))
NN = (((1,), (0,)), ((), ()))
VMEM = pl.BlockSpec(memory_space=pltpu.VMEM)
HBM = pl.BlockSpec(memory_space=pltpu.HBM)
FIRST_LIMIT = 60 * 2**20
LAST_LIMIT = 20 * 2**20
AHEAD = 8


def iota(shape, dim):
    return lax.broadcasted_iota(jnp.int32, shape, dim)


def stay(x):
    return pltpu.with_memory_space_constraint(x, pltpu.HBM)


def up(value, step):
    return -(-value // step) * step


def split(x, parts):
    out = []
    for n in range(parts):
        head = x.astype(BF16)
        out.append(head)
        if n + 1 < parts:
            x = x - head.astype(F32)
    return out


def dot(a, b, dims):
    return lax.dot_general(a, b, dims, preferred_element_type=F32)


def dot_parts(a, b, dims):
    a_hi, a_lo = split(a, 2)
    b_hi, b_lo = split(b, 2)
    rows = a.shape[0]
    both = dot(jnp.concatenate([a_hi, a_lo], axis=0), b_hi, dims)
    return both[:rows] + both[rows:] + dot(a_hi, b_lo, dims)


def dot_exact(a, hot, dims):
    rows = a.shape[0]
    parts = dot(jnp.concatenate(split(a, 3), axis=0), hot, dims)
    return parts[:rows] + parts[rows : 2 * rows] + parts[2 * rows :]


def chunks_of(width):
    for count in (5, 3, 2):
        if width % (count * LANES) == 0:
            return count
    return 1


def rows_of_slots(sub, rhs, lanes):
    return (iota((rhs * sub, lanes), 0) // sub == iota((rhs * sub, lanes), 1)).astype(F32).astype(BF16)


def slab_copies(whole_ref, slabs_ref, sems, back=False):
    count, _, step = slabs_ref.shape
    rows = whole_ref.shape[0] * whole_ref.shape[1]
    flat = whole_ref.reshape(rows, count * step)

    def copy(n):
        part = flat.at[:, pl.ds(n * step, step)]
        slab = slabs_ref.at[n, pl.ds(0, rows)]
        ends = (slab, part) if back else (part, slab)
        return pltpu.make_async_copy(*ends, sems.at[n])

    return copy


def mask_kernel(raw_ref, count_s, size_s, sub):
    rows, width = raw_ref.shape
    slot = iota((rows, width), 0) % sub
    limit = jnp.zeros((rows, width), jnp.int32)
    for s in range(sub):
        size = jnp.where(s < count_s[0, 0], size_s[s], 0)
        limit = jnp.where(slot == s, size, limit)
    return jnp.where(iota((rows, width), 1) < limit, raw_ref[...].astype(F32), 0.0).astype(BF16)


def first_kernel(rhs, counts_ref, sizes_ref, kernel_ref, lower_ref, map_ref, duals_ref,
                 send_ref, inv_ref,
                 count_s, size_s, raw_ref, tri_ref, row_ref, x_ref, acc_ref, mix_ref, block_ref, sol_ref, sems, small_sems):
    modes, sub, width = kernel_ref.shape
    rows = modes * sub
    ck = lower_ref.shape[0]
    lanes = inv_ref.shape[1]
    count, _, step = x_ref.shape
    copy = slab_copies(duals_ref, x_ref, sems)
    small = [
        pltpu.make_async_copy(src, dst, small_sems.at[n])
        for n, (src, dst) in enumerate(
            (
                (lower_ref, tri_ref),
                (map_ref, row_ref),
                (counts_ref, count_s),
                (sizes_ref, size_s),
                (kernel_ref.reshape(rows, width), raw_ref),
            )
        )
    ]
    for one in small:
        one.start()
    for n in range(count):
        copy(n).start()

    place = lax.axis_index("clus").astype(jnp.int32)
    small[0].wait()
    small[1].wait()
    lower = tri_ref[...]
    eye = iota((ck, ck), 0) == iota((ck, ck), 1)
    scale = 1.0 / jnp.sum(jnp.where(eye, lower, 0.0), axis=1, keepdims=True)
    below = jnp.where(iota((ck, ck), 0) > iota((ck, ck), 1), lower * scale, 0.0)
    sol = jnp.where(iota((ck, lanes), 1) == rhs + iota((ck, lanes), 0), scale, 0.0)
    for i in range(ck - 1):
        sol = sol - below[:, i : i + 1] * sol[i : i + 1, :]
    inv_ref[...] = sol
    wanted = iota((rows, ck), 1) == place * rows + iota((rows, ck), 0)
    own_map = jnp.sum(jnp.where(wanted, row_ref[...].astype(F32), 0.0), axis=1, keepdims=True)
    for c in range(lanes // LANES):
        cols = slice(c * LANES, (c + 1) * LANES)
        sol_ref[c] = sol[:, cols]
        block_ref[:, cols] = sol_ref[c, pl.ds(place * rows, rows), :]
    block_ref[...] += jnp.where(iota((rows, lanes), 1) == rhs + ck, own_map, 0.0)

    for one in small[2:]:
        one.wait()
    masked = mask_kernel(raw_ref, count_s, size_s, sub)
    acc_ref[...] = jnp.zeros_like(acc_ref)
    cut = up(rhs * sub // 2, 16)
    halves = [(0, cut), (cut, rhs * sub)]
    sums = [jnp.zeros((rows, stop - start), F32) for start, stop in halves]
    for n in range(count):
        copy(n).wait()
        weight = masked[:, n * step : (n + 1) * step]
        sums = [part + dot(weight, x_ref[n, start:stop, :], NT) for part, (start, stop) in zip(sums, halves)]
    total = jnp.concatenate(sums, axis=1)
    same = iota((rows, rhs * sub), 0) % sub == iota((rows, rhs * sub), 1) % sub
    acc_ref[:rows, :] = jnp.where(same, total, 0.0)
    mixed = dot_exact(acc_ref[...], rows_of_slots(sub, rhs, lanes), NN)
    for c in range(lanes // LANES):
        cols = slice(c * LANES, (c + 1) * LANES)
        mix_ref[c] = mixed[:, cols]
        for s in range(sub):
            here = slice(s * modes, (s + 1) * modes)
            block_ref[here, cols] += mix_ref[c, pl.ds(s, modes, stride=sub), :]
    group = 2 if send_ref.shape[0] % (2 * rows) == 0 else 1
    block = jnp.concatenate([block_ref[...]] * group, axis=0)
    for d in range(send_ref.shape[0] // (rows * group)):
        send_ref[pl.ds(d * rows * group, rows * group), :] = block


def middle_kernel(rhs, inv_ref, picked_ref, counts_ref, sizes_ref, kernel_ref, duals_ref,
                  coarse_ref, turned_ref, x_ref,
                  count_s, size_s, raw_ref, turn_ref, sems, small_sems):
    modes, sub, width = kernel_ref.shape
    rows = modes * sub
    ck = picked_ref.shape[0]
    count, deep, step = x_ref.shape
    flat = duals_ref.shape[0] * sub
    copy = slab_copies(duals_ref, x_ref, sems)
    small = [
        pltpu.make_async_copy(src, dst, small_sems.at[n])
        for n, (src, dst) in enumerate(
            ((counts_ref, count_s), (sizes_ref, size_s), (kernel_ref.reshape(rows, width), raw_ref))
        )
    ]
    for one in small:
        one.start()
    for n in range(count):
        copy(n).start()
    place = lax.axis_index("clus").astype(jnp.int32)
    turn_ref[...] = inv_ref[:, rhs : rhs + ck].T
    turned_ref[...] = jnp.zeros_like(turned_ref)
    for s in range(sub):
        turned_ref[pl.ds(s, modes, stride=sub), :] = turn_ref[pl.ds(place * rows + s * modes, modes), :]
    coarse_ref[...] = lax.dot_general(turned_ref[...], picked_ref[...], NN, precision=HI, preferred_element_type=F32)
    for one in small:
        one.wait()
    masked = mask_kernel(raw_ref, count_s, size_s, sub)
    for n in range(count):
        x_ref[n, flat:, :] = jnp.zeros((deep - flat, step), BF16)
        x_ref[n, flat : flat + rows, :] = masked[:, n * step : (n + 1) * step]
    for n in range(count):
        copy(n).wait()


def write_out(corr, sub, x_ref, out_ref, corr_ref, o_ref, sems):
    flat, rhs = o_ref.shape[1], corr_ref.shape[1]
    count, deep, step = x_ref.shape
    copy = slab_copies(out_ref, o_ref, sems, back=True)
    corr_ref[:flat, :] = jnp.zeros((flat, rhs), BF16)
    corr_ref[flat:, :] = -corr
    wide = dot(rows_of_slots(sub, rhs, rhs), corr_ref[...], NT)
    row, col = iota(wide.shape, 0), iota(wide.shape, 1)
    same = (col >= flat) & (row % sub == col % sub)
    left = jnp.where(same, wide, (row == col).astype(F32)).astype(BF16)
    tile = 2 * LANES if step % (2 * LANES) == 0 else LANES
    tiles = [(n, slice(c, c + tile)) for n in range(count) for c in range(0, step, tile)]
    waiting = []
    for n, cols in [*tiles, *[(None, None)] * AHEAD]:
        if n is not None:
            waiting.append((n, cols, dot(left, x_ref[n, :, cols], NN)))
        if len(waiting) > AHEAD or n is None and waiting:
            done, where, value = waiting.pop(0)
            o_ref[done, :, where] = value.astype(BF16)
            if where.stop == step:
                copy(done).start()
    for n in range(count):
        copy(n).wait()


def block_product(recv_ref, rhs, ck, block_ref):
    total = recv_ref.shape[0]
    block_ref[...] = jnp.zeros_like(block_ref)
    for w in range(total // ck):
        here = slice(w * ck, (w + 1) * ck)
        block_ref[here, here] = recv_ref[here, rhs : rhs + ck]
    spans = []
    for start in range(0, total, LANES):
        stop = min(start + LANES, total)
        low = start // ck * ck // 16 * 16
        high = min(up(up(stop, ck), 16), total)
        spans.append((low, high, dot_parts(block_ref[low:high, start:stop], recv_ref[start:stop, :rhs], NN)))
    return spans


def last_kernel(rhs, sub, recv_ref, coarse_ref, turned_ref, x_ref, out_ref, block_ref, sum_ref, corr_ref, o_ref, sems):
    total = recv_ref.shape[0]
    gk = coarse_ref.shape[1]
    ck = turned_ref.shape[1]
    cluster = lax.axis_index("wide").astype(jnp.int32)
    done = 0
    for low, high, part in block_product(recv_ref, rhs, ck, block_ref):
        if low < done:
            sum_ref[low:done, :] += part[: done - low]
        sum_ref[done:high, :] = part[done - low :]
        done = high
    target = recv_ref[:, rhs + ck : rhs + ck + 1].astype(jnp.int32)
    hot = (target == iota((total, gk), 1)).astype(F32).astype(BF16)
    taken = dot_exact(coarse_ref[...], hot, NT)
    mine = sum_ref[pl.ds(pl.multiple_of(cluster * ck, ck), ck), :]
    corr = dot_parts(turned_ref[...], mine, NN) - dot_parts(taken, sum_ref[...], NN)
    write_out(corr.astype(BF16), sub, x_ref, out_ref, corr_ref, o_ref, sems)


def last_kernel_plain(sub, given_ref, x_ref, out_ref, corr_ref, o_ref, sems):
    write_out(given_ref[...].astype(BF16), sub, x_ref, out_ref, corr_ref, o_ref, sems)


def per_device(duals, kernel, sub_counts, dual_sizes, cluster_factor, coarse_map, coarse_inverse):
    rhs, sub, width = duals.shape
    modes = kernel.shape[1]
    rows = sub * modes
    padded = up(rows, 16)
    clusters = lax.axis_size("wide")
    members = lax.axis_size("clus")
    devices = clusters * members
    total = devices * rows
    ck = cluster_factor.shape[1]
    gk, own_cols = coarse_inverse.shape
    lanes = up(rhs + ck + 1, LANES)
    count = chunks_of(width)
    step = width // count
    place = lax.axis_index("clus").astype(jnp.int32)
    counts = sub_counts.reshape(1, 1)
    sizes = stay(dual_sizes)
    modes_first = stay(kernel.transpose(1, 0, 2))
    vectors = stay(duals)
    slabs = (count, rhs * sub, step)
    deeper = (count, rhs * sub + padded, step)
    small_enough = total * max(total, gk) <= 2**20
    OUT = pltpu.VMEM if small_enough else jax.ShapeDtypeStruct

    send, inv = pl.pallas_call(
        functools.partial(first_kernel, rhs),
        out_shape=(jax.ShapeDtypeStruct((total, lanes), F32), OUT((ck, lanes), F32)),
        in_specs=[HBM] * 6,
        out_specs=(VMEM, VMEM),
        scratch_shapes=[
            pltpu.SMEM((1, 1), jnp.int32),
            pltpu.SMEM((sub,), jnp.int32),
            pltpu.VMEM((rows, width), BF16),
            pltpu.VMEM((ck, ck), F32),
            pltpu.VMEM((1, ck), jnp.int32),
            pltpu.VMEM(slabs, BF16),
            pltpu.VMEM((padded, rhs * sub), F32),
            pltpu.VMEM((lanes // LANES, padded, LANES), F32),
            pltpu.VMEM((rows, lanes), F32),
            pltpu.VMEM((lanes // LANES, ck, LANES), F32),
            pltpu.SemaphoreType.DMA((count,)),
            pltpu.SemaphoreType.DMA((5,)),
        ],
        compiler_params=pltpu.CompilerParams(vmem_limit_bytes=FIRST_LIMIT),
    )(counts, sizes, modes_first, stay(cluster_factor[0]), stay(coarse_map), vectors)

    spread = send.reshape(devices, rows, lanes // LANES, LANES)
    recv = lax.all_to_all(spread, ("wide", "clus"), 0, 0)

    inv, rows_map, coarse_t, _ = lax.optimization_barrier((inv, coarse_map[0], coarse_inverse.T, send))
    hot = (rows_map[:, None] == place * own_cols + iota((ck, own_cols), 1)).astype(F32)
    part = jnp.dot(hot, coarse_t, precision=HI)
    picked = part
    for shift in range(1, members):
        picked = picked + lax.ppermute(part, "clus", [(i, (i + shift) % members) for i in range(members)])
    params = pltpu.CompilerParams(vmem_limit_bytes=LAST_LIMIT)
    coarse, turned, x = pl.pallas_call(
        functools.partial(middle_kernel, rhs),
        out_shape=(
            OUT((padded, gk), F32),
            OUT((padded, ck), F32),
            OUT(deeper, BF16),
        ),
        in_specs=[VMEM, VMEM] + [HBM] * 4,
        out_specs=(VMEM,) * 3,
        scratch_shapes=[
            pltpu.SMEM((1, 1), jnp.int32),
            pltpu.SMEM((sub,), jnp.int32),
            pltpu.VMEM((rows, width), BF16),
            pltpu.VMEM((ck, ck), F32),
            pltpu.SemaphoreType.DMA((count,)),
            pltpu.SemaphoreType.DMA((3,)),
        ],
        compiler_params=params,
    )(inv, picked, counts, sizes, modes_first, vectors)

    out_shape = jax.ShapeDtypeStruct(duals.shape, BF16)
    scratch = [
        pltpu.VMEM((rhs * sub + padded, rhs), BF16),
        pltpu.VMEM(slabs, BF16),
        pltpu.SemaphoreType.DMA((count,)),
    ]
    if small_enough:
        return pl.pallas_call(
            functools.partial(last_kernel, rhs, sub),
            out_shape=out_shape,
            in_specs=[VMEM] * 4,
            out_specs=HBM,
            scratch_shapes=[pltpu.VMEM((total, total), F32), pltpu.VMEM((total, rhs), F32), *scratch],
            compiler_params=params,
        )(recv.reshape(total, lanes), coarse, turned, x)

    blocks = recv.reshape(clusters, ck, lanes)
    forward = jnp.einsum("wam,wmr->war", blocks[:, :, rhs : rhs + ck], blocks[:, :, :rhs], precision=HI)
    target = blocks[:, :, rhs + ck].astype(jnp.int32).reshape(total)
    all_hot = (target[:, None] == iota((total, gk), 1)).astype(F32)
    gsum = lax.dot_general(all_hot, forward.reshape(total, rhs), (((0,), (0,)), ((), ())), precision=HI)
    mine = lax.dynamic_index_in_dim(forward, lax.axis_index("wide"), 0, keepdims=False)
    corr = jnp.dot(turned, mine, precision=HI) - jnp.dot(coarse, gsum, precision=HI)
    return pl.pallas_call(
        functools.partial(last_kernel_plain, sub),
        out_shape=out_shape,
        in_specs=[VMEM] * 2,
        out_specs=HBM,
        scratch_shapes=scratch,
        compiler_params=params,
    )(corr, x)


def solution(mesh):
    in_specs = (
        P(None, ("wide", "clus"), None),
        P(("wide", "clus"), None, None),
        P(("wide", "clus")),
        P(("wide", "clus")),
        P("wide", None, None),
        P("wide", None),
        P(None, "clus"),
    )
    out_specs = P(None, ("wide", "clus"), None)
    return jax.shard_map(
        per_device, mesh=mesh, in_specs=in_specs, out_specs=out_specs, check_vma=False
    )
```

```python
import functools

import jax
import jax.numpy as jnp
from jax import lax
from jax.experimental import pallas as pl
from jax.experimental.pallas import tpu as pltpu
from jax.sharding import PartitionSpec as P

F32 = jnp.float32
BF16 = jnp.bfloat16
LANES = 128
HI = lax.Precision.HIGHEST
NT = (((1,), (1,)), ((), ()))
NN = (((1,), (0,)), ((), ()))
VMEM = pl.BlockSpec(memory_space=pltpu.VMEM)
HBM = pl.BlockSpec(memory_space=pltpu.HBM)
FIRST_LIMIT = 60 * 2**20
LAST_LIMIT = 20 * 2**20
AHEAD = 8


def iota(shape, dim):
    return lax.broadcasted_iota(jnp.int32, shape, dim)


def stay(x):
    return pltpu.with_memory_space_constraint(x, pltpu.HBM)


def up(value, step):
    return -(-value // step) * step


def split(x, parts):
    out = []
    for n in range(parts):
        head = x.astype(BF16)
        out.append(head)
        if n + 1 < parts:
            x = x - head.astype(F32)
    return out


def dot(a, b, dims):
    return lax.dot_general(a, b, dims, preferred_element_type=F32)


def dot_parts(a, b, dims):
    a_hi, a_lo = split(a, 2)
    b_hi, b_lo = split(b, 2)
    rows = a.shape[0]
    both = dot(jnp.concatenate([a_hi, a_lo], axis=0), b_hi, dims)
    return both[:rows] + both[rows:] + dot(a_hi, b_lo, dims)


def dot_exact(a, hot, dims):
    rows = a.shape[0]
    parts = dot(jnp.concatenate(split(a, 3), axis=0), hot, dims)
    return parts[:rows] + parts[rows : 2 * rows] + parts[2 * rows :]


def chunks_of(width):
    for count in (5, 3, 2):
        if width % (count * LANES) == 0:
            return count
    return 1


def tile_of(step):
    return 2 * LANES if step % (2 * LANES) == 0 else LANES


def rows_of_slots(sub, rhs, lanes):
    return (iota((rhs * sub, lanes), 0) // sub == iota((rhs * sub, lanes), 1)).astype(F32).astype(BF16)


def slab_copies(whole_ref, slabs_ref, sems):
    count, _, step = slabs_ref.shape
    rows = whole_ref.shape[0] * whole_ref.shape[1]
    flat = whole_ref.reshape(rows, count * step)

    def copy(n):
        part = flat.at[:, pl.ds(n * step, step)]
        return pltpu.make_async_copy(part, slabs_ref.at[n, pl.ds(0, rows)], sems.at[n])

    return copy


def mask_kernel(raw_ref, count_s, size_s, sub):
    rows, width = raw_ref.shape
    slot = iota((rows, width), 0) % sub
    limit = jnp.zeros((rows, width), jnp.int32)
    for s in range(sub):
        size = jnp.where(s < count_s[0, 0], size_s[s], 0)
        limit = jnp.where(slot == s, size, limit)
    return jnp.where(iota((rows, width), 1) < limit, raw_ref[...].astype(F32), 0.0).astype(BF16)


def first_kernel(rhs, counts_ref, sizes_ref, kernel_ref, lower_ref, map_ref, duals_ref,
                 send_ref, inv_ref,
                 count_s, size_s, raw_ref, tri_ref, row_ref, x_ref, acc_ref, mix_ref, block_ref, sol_ref, sems, small_sems):
    modes, sub, width = kernel_ref.shape
    rows = modes * sub
    ck = lower_ref.shape[0]
    lanes = inv_ref.shape[1]
    count, _, step = x_ref.shape
    copy = slab_copies(duals_ref, x_ref, sems)
    small = [
        pltpu.make_async_copy(src, dst, small_sems.at[n])
        for n, (src, dst) in enumerate(
            (
                (lower_ref, tri_ref),
                (map_ref, row_ref),
                (counts_ref, count_s),
                (sizes_ref, size_s),
                (kernel_ref.reshape(rows, width), raw_ref),
            )
        )
    ]
    for one in small:
        one.start()
    for n in range(count):
        copy(n).start()

    place = lax.axis_index("clus").astype(jnp.int32)
    small[0].wait()
    small[1].wait()
    lower = tri_ref[...]
    eye = iota((ck, ck), 0) == iota((ck, ck), 1)
    scale = 1.0 / jnp.sum(jnp.where(eye, lower, 0.0), axis=1, keepdims=True)
    below = jnp.where(iota((ck, ck), 0) > iota((ck, ck), 1), lower * scale, 0.0)
    sol = jnp.where(iota((ck, lanes), 1) == rhs + iota((ck, lanes), 0), scale, 0.0)
    for i in range(ck - 1):
        sol = sol - below[:, i : i + 1] * sol[i : i + 1, :]
    inv_ref[...] = sol
    wanted = iota((rows, ck), 1) == place * rows + iota((rows, ck), 0)
    own_map = jnp.sum(jnp.where(wanted, row_ref[...].astype(F32), 0.0), axis=1, keepdims=True)
    for c in range(lanes // LANES):
        cols = slice(c * LANES, (c + 1) * LANES)
        sol_ref[c] = sol[:, cols]
        block_ref[:, cols] = sol_ref[c, pl.ds(place * rows, rows), :]
    block_ref[...] += jnp.where(iota((rows, lanes), 1) == rhs + ck, own_map, 0.0)

    for one in small[2:]:
        one.wait()
    masked = mask_kernel(raw_ref, count_s, size_s, sub)
    acc_ref[...] = jnp.zeros_like(acc_ref)
    cut = up(rhs * sub // 2, 16)
    halves = [(0, cut), (cut, rhs * sub)]
    sums = [jnp.zeros((rows, stop - start), F32) for start, stop in halves]
    for n in range(count):
        copy(n).wait()
        weight = masked[:, n * step : (n + 1) * step]
        sums = [part + dot(weight, x_ref[n, start:stop, :], NT) for part, (start, stop) in zip(sums, halves)]
    total = jnp.concatenate(sums, axis=1)
    same = iota((rows, rhs * sub), 0) % sub == iota((rows, rhs * sub), 1) % sub
    acc_ref[:rows, :] = jnp.where(same, total, 0.0)
    mixed = dot_exact(acc_ref[...], rows_of_slots(sub, rhs, lanes), NN)
    for c in range(lanes // LANES):
        cols = slice(c * LANES, (c + 1) * LANES)
        mix_ref[c] = mixed[:, cols]
        for s in range(sub):
            here = slice(s * modes, (s + 1) * modes)
            block_ref[here, cols] += mix_ref[c, pl.ds(s, modes, stride=sub), :]
    group = 2 if send_ref.shape[0] % (2 * rows) == 0 else 1
    block = jnp.concatenate([block_ref[...]] * group, axis=0)
    for d in range(send_ref.shape[0] // (rows * group)):
        send_ref[pl.ds(d * rows * group, rows * group), :] = block


def middle_kernel(rhs, inv_ref, picked_ref, counts_ref, sizes_ref, kernel_ref, duals_ref,
                  coarse_ref, turned_ref, x_ref,
                  count_s, size_s, raw_ref, turn_ref, sems, small_sems):
    modes, sub, width = kernel_ref.shape
    rows = modes * sub
    ck = picked_ref.shape[0]
    count, deep, step = x_ref.shape
    flat = duals_ref.shape[0] * sub
    copy = slab_copies(duals_ref, x_ref, sems)
    small = [
        pltpu.make_async_copy(src, dst, small_sems.at[n])
        for n, (src, dst) in enumerate(
            ((counts_ref, count_s), (sizes_ref, size_s), (kernel_ref.reshape(rows, width), raw_ref))
        )
    ]
    for one in small:
        one.start()
    for n in range(count):
        copy(n).start()
    place = lax.axis_index("clus").astype(jnp.int32)
    turn_ref[...] = inv_ref[:, rhs : rhs + ck].T
    turned_ref[...] = jnp.zeros_like(turned_ref)
    for s in range(sub):
        turned_ref[pl.ds(s, modes, stride=sub), :] = turn_ref[pl.ds(place * rows + s * modes, modes), :]
    coarse_ref[...] = lax.dot_general(turned_ref[...], picked_ref[...], NN, precision=HI, preferred_element_type=F32)
    for one in small:
        one.wait()
    masked = mask_kernel(raw_ref, count_s, size_s, sub)
    for n in range(count):
        x_ref[n, flat:, :] = jnp.zeros((deep - flat, step), BF16)
        x_ref[n, flat : flat + rows, :] = masked[:, n * step : (n + 1) * step]
    for n in range(count):
        copy(n).wait()


def write_out(corr, sub, x_ref, out_ref, corr_ref, o_ref, sems):
    flat, rhs = o_ref.shape[1], corr_ref.shape[1]
    count, deep, step = x_ref.shape
    base = flat // LANES * LANES
    corr_ref[: flat - base, :] = jnp.zeros((flat - base, rhs), BF16)
    corr_ref[flat - base :, :] = -corr
    wide = dot(rows_of_slots(sub, rhs, rhs), corr_ref[...], NT)
    row, col = iota(wide.shape, 0), iota(wide.shape, 1) + base
    same = (col >= flat) & (row % sub == col % sub)
    left = jnp.where(same, wide, (row == col).astype(F32)).astype(BF16)
    if base:
        eye = (iota((flat, base), 0) == iota((flat, base), 1)).astype(F32).astype(BF16)
        left = jnp.concatenate([eye, left], axis=1)
    tile = tile_of(step)
    out_flat = out_ref.reshape(flat, count * step)

    def copy(n, cols):
        part = out_flat.at[:, pl.ds(n * step + cols.start, tile)]
        return pltpu.make_async_copy(o_ref.at[n, :, cols], part, sems.at[n, cols.start // tile])

    tiles = [(n, slice(c, c + tile)) for n in range(count) for c in range(0, step, tile)]
    waiting = []
    for n, cols in [*tiles, *[(None, None)] * AHEAD]:
        if n is not None:
            waiting.append((n, cols, dot(left, x_ref[n, :, cols], NN)))
        if len(waiting) > AHEAD or n is None and waiting:
            done, where, value = waiting.pop(0)
            o_ref[done, :, where] = value.astype(BF16)
            copy(done, where).start()
    for n, cols in tiles:
        copy(n, cols).wait()


def block_product(recv_ref, rhs, ck, block_ref):
    total = recv_ref.shape[0]
    block_ref[...] = jnp.zeros_like(block_ref)
    for w in range(total // ck):
        here = slice(w * ck, (w + 1) * ck)
        block_ref[here, here] = recv_ref[here, rhs : rhs + ck]
    spans = []
    for start in range(0, total, LANES):
        stop = min(start + LANES, total)
        low = start // ck * ck // 16 * 16
        high = min(up(up(stop, ck), 16), total)
        spans.append((low, high, dot_parts(block_ref[low:high, start:stop], recv_ref[start:stop, :rhs], NN)))
    return spans


def last_kernel(rhs, sub, recv_ref, coarse_ref, turned_ref, x_ref, out_ref, block_ref, sum_ref, corr_ref, o_ref, sems):
    total = recv_ref.shape[0]
    gk = coarse_ref.shape[1]
    ck = turned_ref.shape[1]
    cluster = lax.axis_index("wide").astype(jnp.int32)
    done = 0
    for low, high, part in block_product(recv_ref, rhs, ck, block_ref):
        if low < done:
            sum_ref[low:done, :] += part[: done - low]
        sum_ref[done:high, :] = part[done - low :]
        done = high
    target = recv_ref[:, rhs + ck : rhs + ck + 1].astype(jnp.int32)
    hot = (target == iota((total, gk), 1)).astype(F32).astype(BF16)
    taken = dot_exact(coarse_ref[...], hot, NT)
    mine = sum_ref[pl.ds(pl.multiple_of(cluster * ck, ck), ck), :]
    corr = dot_parts(turned_ref[...], mine, NN) - dot_parts(taken, sum_ref[...], NN)
    write_out(corr.astype(BF16), sub, x_ref, out_ref, corr_ref, o_ref, sems)


def last_kernel_plain(sub, given_ref, x_ref, out_ref, corr_ref, o_ref, sems):
    write_out(given_ref[...].astype(BF16), sub, x_ref, out_ref, corr_ref, o_ref, sems)


def per_device(duals, kernel, sub_counts, dual_sizes, cluster_factor, coarse_map, coarse_inverse):
    rhs, sub, width = duals.shape
    modes = kernel.shape[1]
    rows = sub * modes
    padded = up(rows, 16)
    clusters = lax.axis_size("wide")
    members = lax.axis_size("clus")
    devices = clusters * members
    total = devices * rows
    ck = cluster_factor.shape[1]
    gk, own_cols = coarse_inverse.shape
    lanes = up(rhs + ck + 1, LANES)
    count = chunks_of(width)
    step = width // count
    place = lax.axis_index("clus").astype(jnp.int32)
    counts = sub_counts.reshape(1, 1)
    sizes = stay(dual_sizes)
    modes_first = stay(kernel.transpose(1, 0, 2))
    vectors = stay(duals)
    slabs = (count, rhs * sub, step)
    deeper = (count, rhs * sub + padded, step)
    small_enough = total * max(total, gk) <= 2**20
    OUT = pltpu.VMEM if small_enough else jax.ShapeDtypeStruct

    send, inv = pl.pallas_call(
        functools.partial(first_kernel, rhs),
        out_shape=(jax.ShapeDtypeStruct((total, lanes), F32), OUT((ck, lanes), F32)),
        in_specs=[HBM] * 6,
        out_specs=(VMEM, VMEM),
        scratch_shapes=[
            pltpu.SMEM((1, 1), jnp.int32),
            pltpu.SMEM((sub,), jnp.int32),
            pltpu.VMEM((rows, width), BF16),
            pltpu.VMEM((ck, ck), F32),
            pltpu.VMEM((1, ck), jnp.int32),
            pltpu.VMEM(slabs, BF16),
            pltpu.VMEM((padded, rhs * sub), F32),
            pltpu.VMEM((lanes // LANES, padded, LANES), F32),
            pltpu.VMEM((rows, lanes), F32),
            pltpu.VMEM((lanes // LANES, ck, LANES), F32),
            pltpu.SemaphoreType.DMA((count,)),
            pltpu.SemaphoreType.DMA((5,)),
        ],
        compiler_params=pltpu.CompilerParams(vmem_limit_bytes=FIRST_LIMIT),
    )(counts, sizes, modes_first, stay(cluster_factor[0]), stay(coarse_map), vectors)

    spread = send.reshape(devices, rows, lanes // LANES, LANES)
    recv = lax.all_to_all(spread, ("wide", "clus"), 0, 0)

    inv, rows_map, coarse_t, _ = lax.optimization_barrier((inv, coarse_map[0], coarse_inverse.T, send))
    hot = (rows_map[:, None] == place * own_cols + iota((ck, own_cols), 1)).astype(F32)
    part = jnp.dot(hot, coarse_t, precision=HI)
    picked = part
    for shift in range(1, members):
        picked = picked + lax.ppermute(part, "clus", [(i, (i + shift) % members) for i in range(members)])
    params = pltpu.CompilerParams(vmem_limit_bytes=LAST_LIMIT)
    coarse, turned, x = pl.pallas_call(
        functools.partial(middle_kernel, rhs),
        out_shape=(
            OUT((padded, gk), F32),
            OUT((padded, ck), F32),
            OUT(deeper, BF16),
        ),
        in_specs=[VMEM, VMEM] + [HBM] * 4,
        out_specs=(VMEM,) * 3,
        scratch_shapes=[
            pltpu.SMEM((1, 1), jnp.int32),
            pltpu.SMEM((sub,), jnp.int32),
            pltpu.VMEM((rows, width), BF16),
            pltpu.VMEM((ck, ck), F32),
            pltpu.SemaphoreType.DMA((count,)),
            pltpu.SemaphoreType.DMA((3,)),
        ],
        compiler_params=params,
    )(inv, picked, counts, sizes, modes_first, vectors)

    out_shape = jax.ShapeDtypeStruct(duals.shape, BF16)
    scratch = [
        pltpu.VMEM((rhs * sub % LANES + padded, rhs), BF16),
        pltpu.VMEM(slabs, BF16),
        pltpu.SemaphoreType.DMA((count, step // tile_of(step))),
    ]
    if small_enough:
        return pl.pallas_call(
            functools.partial(last_kernel, rhs, sub),
            out_shape=out_shape,
            in_specs=[VMEM] * 4,
            out_specs=HBM,
            scratch_shapes=[pltpu.VMEM((total, total), F32), pltpu.VMEM((total, rhs), F32), *scratch],
            compiler_params=params,
        )(recv.reshape(total, lanes), coarse, turned, x)

    blocks = recv.reshape(clusters, ck, lanes)
    forward = jnp.einsum("wam,wmr->war", blocks[:, :, rhs : rhs + ck], blocks[:, :, :rhs], precision=HI)
    target = blocks[:, :, rhs + ck].astype(jnp.int32).reshape(total)
    all_hot = (target[:, None] == iota((total, gk), 1)).astype(F32)
    gsum = lax.dot_general(all_hot, forward.reshape(total, rhs), (((0,), (0,)), ((), ())), precision=HI)
    mine = lax.dynamic_index_in_dim(forward, lax.axis_index("wide"), 0, keepdims=False)
    corr = jnp.dot(turned, mine, precision=HI) - jnp.dot(coarse, gsum, precision=HI)
    return pl.pallas_call(
        functools.partial(last_kernel_plain, sub),
        out_shape=out_shape,
        in_specs=[VMEM] * 2,
        out_specs=HBM,
        scratch_shapes=scratch,
        compiler_params=params,
    )(corr, x)


def solution(mesh):
    in_specs = (
        P(None, ("wide", "clus"), None),
        P(("wide", "clus"), None, None),
        P(("wide", "clus")),
        P(("wide", "clus")),
        P("wide", None, None),
        P("wide", None),
        P(None, "clus"),
    )
    out_specs = P(None, ("wide", "clus"), None)
    return jax.shard_map(
        per_device, mesh=mesh, in_specs=in_specs, out_specs=out_specs, check_vma=False
    )
```

```python
import functools

import jax
import jax.numpy as jnp
from jax import lax
from jax.experimental import pallas as pl
from jax.experimental.pallas import tpu as pltpu
from jax.sharding import PartitionSpec as P

F32 = jnp.float32
BF16 = jnp.bfloat16
LANES = 128
HI = lax.Precision.HIGHEST
NT = (((1,), (1,)), ((), ()))
NN = (((1,), (0,)), ((), ()))
VMEM = pl.BlockSpec(memory_space=pltpu.VMEM)
HBM = pl.BlockSpec(memory_space=pltpu.HBM)
FIRST_LIMIT = 60 * 2**20
LAST_LIMIT = 20 * 2**20
AHEAD = 8


def iota(shape, dim):
    return lax.broadcasted_iota(jnp.int32, shape, dim)


def stay(x):
    return pltpu.with_memory_space_constraint(x, pltpu.HBM)


def up(value, step):
    return -(-value // step) * step


def split(x, parts):
    out = []
    for n in range(parts):
        head = x.astype(BF16)
        out.append(head)
        if n + 1 < parts:
            x = x - head.astype(F32)
    return out


def dot(a, b, dims):
    return lax.dot_general(a, b, dims, preferred_element_type=F32)


def dot_parts(a, b, dims):
    a_hi, a_lo = split(a, 2)
    b_hi, b_lo = split(b, 2)
    rows = a.shape[0]
    both = dot(jnp.concatenate([a_hi, a_lo], axis=0), b_hi, dims)
    return both[:rows] + both[rows:] + dot(a_hi, b_lo, dims)


def dot_exact(a, hot, dims):
    rows = a.shape[0]
    parts = dot(jnp.concatenate(split(a, 3), axis=0), hot, dims)
    return parts[:rows] + parts[rows : 2 * rows] + parts[2 * rows :]


def chunks_of(width):
    for count in (5, 3, 2):
        if width % (count * LANES) == 0:
            return count
    return 1


def tile_of(step):
    return 2 * LANES if step % (2 * LANES) == 0 else LANES


def rows_of_slots(sub, rhs, lanes):
    return (iota((rhs * sub, lanes), 0) // sub == iota((rhs * sub, lanes), 1)).astype(F32).astype(BF16)


def slab_copies(whole_ref, slabs_ref, sems):
    count, _, step = slabs_ref.shape
    rows = whole_ref.shape[0] * whole_ref.shape[1]
    flat = whole_ref.reshape(rows, count * step)

    def copy(n):
        part = flat.at[:, pl.ds(n * step, step)]
        return pltpu.make_async_copy(part, slabs_ref.at[n, pl.ds(0, rows)], sems.at[n])

    return copy


def mask_kernel(raw_ref, count_s, size_s, sub):
    rows, width = raw_ref.shape
    slot = iota((rows, width), 0) % sub
    limit = jnp.zeros((rows, width), jnp.int32)
    for s in range(sub):
        size = jnp.where(s < count_s[0, 0], size_s[s], 0)
        limit = jnp.where(slot == s, size, limit)
    return jnp.where(iota((rows, width), 1) < limit, raw_ref[...].astype(F32), 0.0).astype(BF16)


def first_kernel(rhs, counts_ref, sizes_ref, kernel_ref, lower_ref, map_ref, duals_ref,
                 send_ref, inv_ref, x_ref,
                 count_s, size_s, raw_ref, tri_ref, row_ref, acc_ref, mix_ref, block_ref, sol_ref, sems, small_sems):
    modes, sub, width = kernel_ref.shape
    rows = modes * sub
    ck = lower_ref.shape[0]
    lanes = inv_ref.shape[1]
    count, deep, step = x_ref.shape
    flat = rhs * sub
    copy = slab_copies(duals_ref, x_ref, sems)
    small = [
        pltpu.make_async_copy(src, dst, small_sems.at[n])
        for n, (src, dst) in enumerate(
            (
                (lower_ref, tri_ref),
                (map_ref, row_ref),
                (counts_ref, count_s),
                (sizes_ref, size_s),
                (kernel_ref.reshape(rows, width), raw_ref),
            )
        )
    ]
    for one in small:
        one.start()
    for n in range(count):
        copy(n).start()

    place = lax.axis_index("clus").astype(jnp.int32)
    small[0].wait()
    small[1].wait()
    lower = tri_ref[...]
    eye = iota((ck, ck), 0) == iota((ck, ck), 1)
    scale = 1.0 / jnp.sum(jnp.where(eye, lower, 0.0), axis=1, keepdims=True)
    below = jnp.where(iota((ck, ck), 0) > iota((ck, ck), 1), lower * scale, 0.0)
    sol = jnp.where(iota((ck, lanes), 1) == rhs + iota((ck, lanes), 0), scale, 0.0)
    for i in range(ck - 1):
        sol = sol - below[:, i : i + 1] * sol[i : i + 1, :]
    inv_ref[...] = sol
    wanted = iota((rows, ck), 1) == place * rows + iota((rows, ck), 0)
    own_map = jnp.sum(jnp.where(wanted, row_ref[...].astype(F32), 0.0), axis=1, keepdims=True)
    for c in range(lanes // LANES):
        cols = slice(c * LANES, (c + 1) * LANES)
        sol_ref[c] = sol[:, cols]
        block_ref[:, cols] = sol_ref[c, pl.ds(place * rows, rows), :]
    block_ref[...] += jnp.where(iota((rows, lanes), 1) == rhs + ck, own_map, 0.0)

    for one in small[2:]:
        one.wait()
    masked = mask_kernel(raw_ref, count_s, size_s, sub)
    for n in range(count):
        x_ref[n, flat:, :] = jnp.zeros((deep - flat, step), BF16)
        x_ref[n, flat : flat + rows, :] = masked[:, n * step : (n + 1) * step]
    acc_ref[...] = jnp.zeros_like(acc_ref)
    cut = up(rhs * sub // 2, 16)
    halves = [(0, cut), (cut, rhs * sub)]
    sums = [jnp.zeros((rows, stop - start), F32) for start, stop in halves]
    for n in range(count):
        copy(n).wait()
        weight = masked[:, n * step : (n + 1) * step]
        sums = [part + dot(weight, x_ref[n, start:stop, :], NT) for part, (start, stop) in zip(sums, halves)]
    total = jnp.concatenate(sums, axis=1)
    same = iota((rows, rhs * sub), 0) % sub == iota((rows, rhs * sub), 1) % sub
    acc_ref[:rows, :] = jnp.where(same, total, 0.0)
    mixed = dot_exact(acc_ref[...], rows_of_slots(sub, rhs, lanes), NN)
    for c in range(lanes // LANES):
        cols = slice(c * LANES, (c + 1) * LANES)
        mix_ref[c] = mixed[:, cols]
        for s in range(sub):
            here = slice(s * modes, (s + 1) * modes)
            block_ref[here, cols] += mix_ref[c, pl.ds(s, modes, stride=sub), :]
    group = 2 if send_ref.shape[0] % (2 * rows) == 0 else 1
    block = jnp.concatenate([block_ref[...]] * group, axis=0)
    for d in range(send_ref.shape[0] // (rows * group)):
        send_ref[pl.ds(d * rows * group, rows * group), :] = block


def middle_kernel(rhs, sub, inv_ref, picked_ref, coarse_ref, turned_ref, turn_ref):
    ck = picked_ref.shape[0]
    rows = ck // lax.axis_size("clus")
    modes = rows // sub
    place = lax.axis_index("clus").astype(jnp.int32)
    turn_ref[...] = inv_ref[:, rhs : rhs + ck].T
    turned_ref[...] = jnp.zeros_like(turned_ref)
    for s in range(sub):
        turned_ref[pl.ds(s, modes, stride=sub), :] = turn_ref[pl.ds(place * rows + s * modes, modes), :]
    coarse_ref[...] = lax.dot_general(turned_ref[...], picked_ref[...], NN, precision=HI, preferred_element_type=F32)


def write_out(corr, sub, x_ref, out_ref, corr_ref, o_ref, sems):
    flat, rhs = o_ref.shape[1], corr_ref.shape[1]
    count, deep, step = x_ref.shape
    base = flat // LANES * LANES
    corr_ref[: flat - base, :] = jnp.zeros((flat - base, rhs), BF16)
    corr_ref[flat - base :, :] = -corr
    wide = dot(rows_of_slots(sub, rhs, rhs), corr_ref[...], NT)
    row, col = iota(wide.shape, 0), iota(wide.shape, 1) + base
    same = (col >= flat) & (row % sub == col % sub)
    left = jnp.where(same, wide, (row == col).astype(F32)).astype(BF16)
    if base:
        eye = (iota((flat, base), 0) == iota((flat, base), 1)).astype(F32).astype(BF16)
        left = jnp.concatenate([eye, left], axis=1)
    tile = tile_of(step)
    out_flat = out_ref.reshape(flat, count * step)

    def copy(n, cols):
        part = out_flat.at[:, pl.ds(n * step + cols.start, tile)]
        return pltpu.make_async_copy(o_ref.at[n, :, cols], part, sems.at[n, cols.start // tile])

    tiles = [(n, slice(c, c + tile)) for n in range(count) for c in range(0, step, tile)]
    waiting = []
    for n, cols in [*tiles, *[(None, None)] * AHEAD]:
        if n is not None:
            waiting.append((n, cols, dot(left, x_ref[n, :, cols], NN)))
        if len(waiting) > AHEAD or n is None and waiting:
            done, where, value = waiting.pop(0)
            o_ref[done, :, where] = value.astype(BF16)
            copy(done, where).start()
    for n, cols in tiles:
        copy(n, cols).wait()


def block_product(recv_ref, rhs, ck, block_ref):
    total = recv_ref.shape[0]
    block_ref[...] = jnp.zeros_like(block_ref)
    for w in range(total // ck):
        here = slice(w * ck, (w + 1) * ck)
        block_ref[here, here] = recv_ref[here, rhs : rhs + ck]
    spans = []
    for start in range(0, total, LANES):
        stop = min(start + LANES, total)
        low = start // ck * ck // 16 * 16
        high = min(up(up(stop, ck), 16), total)
        spans.append((low, high, dot_parts(block_ref[low:high, start:stop], recv_ref[start:stop, :rhs], NN)))
    return spans


def last_kernel(rhs, sub, recv_ref, coarse_ref, turned_ref, x_ref, out_ref, block_ref, sum_ref, corr_ref, o_ref, sems):
    total = recv_ref.shape[0]
    gk = coarse_ref.shape[1]
    ck = turned_ref.shape[1]
    cluster = lax.axis_index("wide").astype(jnp.int32)
    done = 0
    for low, high, part in block_product(recv_ref, rhs, ck, block_ref):
        if low < done:
            sum_ref[low:done, :] += part[: done - low]
        sum_ref[done:high, :] = part[done - low :]
        done = high
    target = recv_ref[:, rhs + ck : rhs + ck + 1].astype(jnp.int32)
    hot = (target == iota((total, gk), 1)).astype(F32).astype(BF16)
    taken = dot_exact(coarse_ref[...], hot, NT)
    mine = sum_ref[pl.ds(pl.multiple_of(cluster * ck, ck), ck), :]
    corr = dot_parts(turned_ref[...], mine, NN) - dot_parts(taken, sum_ref[...], NN)
    write_out(corr.astype(BF16), sub, x_ref, out_ref, corr_ref, o_ref, sems)


def last_kernel_plain(sub, given_ref, x_ref, out_ref, corr_ref, o_ref, sems):
    write_out(given_ref[...].astype(BF16), sub, x_ref, out_ref, corr_ref, o_ref, sems)


def per_device(duals, kernel, sub_counts, dual_sizes, cluster_factor, coarse_map, coarse_inverse):
    rhs, sub, width = duals.shape
    modes = kernel.shape[1]
    rows = sub * modes
    padded = up(rows, 16)
    clusters = lax.axis_size("wide")
    members = lax.axis_size("clus")
    devices = clusters * members
    total = devices * rows
    ck = cluster_factor.shape[1]
    gk, own_cols = coarse_inverse.shape
    lanes = up(rhs + ck + 1, LANES)
    count = chunks_of(width)
    step = width // count
    place = lax.axis_index("clus").astype(jnp.int32)
    counts = sub_counts.reshape(1, 1)
    sizes = stay(dual_sizes)
    modes_first = stay(kernel.transpose(1, 0, 2))
    vectors = stay(duals)
    slabs = (count, rhs * sub, step)
    deeper = (count, rhs * sub + padded, step)
    small_enough = total * max(total, gk) <= 2**20
    OUT = pltpu.VMEM if small_enough else jax.ShapeDtypeStruct

    send, inv, x = pl.pallas_call(
        functools.partial(first_kernel, rhs),
        out_shape=(jax.ShapeDtypeStruct((total, lanes), F32), OUT((ck, lanes), F32), OUT(deeper, BF16)),
        in_specs=[HBM] * 6,
        out_specs=(VMEM, VMEM, VMEM),
        scratch_shapes=[
            pltpu.SMEM((1, 1), jnp.int32),
            pltpu.SMEM((sub,), jnp.int32),
            pltpu.VMEM((rows, width), BF16),
            pltpu.VMEM((ck, ck), F32),
            pltpu.VMEM((1, ck), jnp.int32),
            pltpu.VMEM((padded, rhs * sub), F32),
            pltpu.VMEM((lanes // LANES, padded, LANES), F32),
            pltpu.VMEM((rows, lanes), F32),
            pltpu.VMEM((lanes // LANES, ck, LANES), F32),
            pltpu.SemaphoreType.DMA((count,)),
            pltpu.SemaphoreType.DMA((5,)),
        ],
        compiler_params=pltpu.CompilerParams(vmem_limit_bytes=FIRST_LIMIT),
    )(counts, sizes, modes_first, stay(cluster_factor[0]), stay(coarse_map), vectors)

    spread = send.reshape(devices, rows, lanes // LANES, LANES)
    recv = lax.all_to_all(spread, ("wide", "clus"), 0, 0)

    inv, rows_map, coarse_t, _ = lax.optimization_barrier((inv, coarse_map[0], coarse_inverse.T, send))
    hot = (rows_map[:, None] == place * own_cols + iota((ck, own_cols), 1)).astype(F32)
    part = jnp.dot(hot, coarse_t, precision=HI)
    picked = part
    for shift in range(1, members):
        picked = picked + lax.ppermute(part, "clus", [(i, (i + shift) % members) for i in range(members)])
    params = pltpu.CompilerParams(vmem_limit_bytes=LAST_LIMIT)
    coarse, turned = pl.pallas_call(
        functools.partial(middle_kernel, rhs, sub),
        out_shape=(OUT((padded, gk), F32), OUT((padded, ck), F32)),
        in_specs=[VMEM, VMEM],
        out_specs=(VMEM, VMEM),
        scratch_shapes=[pltpu.VMEM((ck, ck), F32)],
        compiler_params=params,
    )(inv, picked)

    out_shape = jax.ShapeDtypeStruct(duals.shape, BF16)
    scratch = [
        pltpu.VMEM((rhs * sub % LANES + padded, rhs), BF16),
        pltpu.VMEM(slabs, BF16),
        pltpu.SemaphoreType.DMA((count, step // tile_of(step))),
    ]
    if small_enough:
        return pl.pallas_call(
            functools.partial(last_kernel, rhs, sub),
            out_shape=out_shape,
            in_specs=[VMEM] * 4,
            out_specs=HBM,
            scratch_shapes=[pltpu.VMEM((total, total), F32), pltpu.VMEM((total, rhs), F32), *scratch],
            compiler_params=params,
        )(recv.reshape(total, lanes), coarse, turned, x)

    blocks = recv.reshape(clusters, ck, lanes)
    forward = jnp.einsum("wam,wmr->war", blocks[:, :, rhs : rhs + ck], blocks[:, :, :rhs], precision=HI)
    target = blocks[:, :, rhs + ck].astype(jnp.int32).reshape(total)
    all_hot = (target[:, None] == iota((total, gk), 1)).astype(F32)
    gsum = lax.dot_general(all_hot, forward.reshape(total, rhs), (((0,), (0,)), ((), ())), precision=HI)
    mine = lax.dynamic_index_in_dim(forward, lax.axis_index("wide"), 0, keepdims=False)
    corr = jnp.dot(turned, mine, precision=HI) - jnp.dot(coarse, gsum, precision=HI)
    return pl.pallas_call(
        functools.partial(last_kernel_plain, sub),
        out_shape=out_shape,
        in_specs=[VMEM] * 2,
        out_specs=HBM,
        scratch_shapes=scratch,
        compiler_params=params,
    )(corr, x)


def solution(mesh):
    in_specs = (
        P(None, ("wide", "clus"), None),
        P(("wide", "clus"), None, None),
        P(("wide", "clus")),
        P(("wide", "clus")),
        P("wide", None, None),
        P("wide", None),
        P(None, "clus"),
    )
    out_specs = P(None, ("wide", "clus"), None)
    return jax.shard_map(
        per_device, mesh=mesh, in_specs=in_specs, out_specs=out_specs, check_vma=False
    )
```

```python
import functools

import jax
import jax.numpy as jnp
from jax import lax
from jax.experimental import pallas as pl
from jax.experimental.pallas import tpu as pltpu
from jax.sharding import PartitionSpec as P

F32 = jnp.float32
BF16 = jnp.bfloat16
LANES = 128
HI = lax.Precision.HIGHEST
NT = (((1,), (1,)), ((), ()))
NN = (((1,), (0,)), ((), ()))
VMEM = pl.BlockSpec(memory_space=pltpu.VMEM)
HBM = pl.BlockSpec(memory_space=pltpu.HBM)
FIRST_LIMIT = 60 * 2**20
LAST_LIMIT = 20 * 2**20
AHEAD = 6


def iota(shape, dim):
    return lax.broadcasted_iota(jnp.int32, shape, dim)


def stay(x):
    return pltpu.with_memory_space_constraint(x, pltpu.HBM)


def up(value, step):
    return -(-value // step) * step


def split(x, parts):
    out = []
    for n in range(parts):
        head = x.astype(BF16)
        out.append(head)
        if n + 1 < parts:
            x = x - head.astype(F32)
    return out


def dot(a, b, dims):
    return lax.dot_general(a, b, dims, preferred_element_type=F32)


def dot_parts(a, b, dims):
    a_hi, a_lo = split(a, 2)
    b_hi, b_lo = split(b, 2)
    rows = a.shape[0]
    both = dot(jnp.concatenate([a_hi, a_lo], axis=0), b_hi, dims)
    return both[:rows] + both[rows:] + dot(a_hi, b_lo, dims)


def dot_exact(a, hot, dims):
    rows = a.shape[0]
    parts = dot(jnp.concatenate(split(a, 3), axis=0), hot, dims)
    return parts[:rows] + parts[rows : 2 * rows] + parts[2 * rows :]


def chunks_of(width):
    for count in (5, 3, 2):
        if width % (count * LANES) == 0:
            return count
    return 1


def tile_of(step):
    return 2 * LANES if step % (2 * LANES) == 0 else LANES


def rows_of_slots(sub, rhs, lanes):
    return (iota((rhs * sub, lanes), 0) // sub == iota((rhs * sub, lanes), 1)).astype(F32).astype(BF16)


def slab_copies(whole_ref, slabs_ref, sems):
    count, _, step = slabs_ref.shape
    rows = whole_ref.shape[0] * whole_ref.shape[1]
    flat = whole_ref.reshape(rows, count * step)

    def copy(n):
        part = flat.at[:, pl.ds(n * step, step)]
        return pltpu.make_async_copy(part, slabs_ref.at[n, pl.ds(0, rows)], sems.at[n])

    return copy


def mask_kernel(raw_ref, count_s, size_s, sub):
    rows, width = raw_ref.shape
    slot = iota((rows, width), 0) % sub
    limit = jnp.zeros((rows, width), jnp.int32)
    for s in range(sub):
        size = jnp.where(s < count_s[0, 0], size_s[s], 0)
        limit = jnp.where(slot == s, size, limit)
    return jnp.where(iota((rows, width), 1) < limit, raw_ref[...].astype(F32), 0.0).astype(BF16)


def first_kernel(rhs, counts_ref, sizes_ref, kernel_ref, lower_ref, map_ref, duals_ref,
                 send_ref, inv_ref, x_ref,
                 count_s, size_s, raw_ref, tri_ref, row_ref, acc_ref, block_ref, sol_ref, sems, small_sems):
    modes, sub, width = kernel_ref.shape
    rows = modes * sub
    ck = lower_ref.shape[0]
    lanes = inv_ref.shape[1]
    count, deep, step = x_ref.shape
    flat = rhs * sub
    copy = slab_copies(duals_ref, x_ref, sems)
    small = [
        pltpu.make_async_copy(src, dst, small_sems.at[n])
        for n, (src, dst) in enumerate(
            (
                (lower_ref, tri_ref),
                (map_ref, row_ref),
                (counts_ref, count_s),
                (sizes_ref, size_s),
                (kernel_ref.reshape(rows, width), raw_ref),
            )
        )
    ]
    for one in small:
        one.start()
    for n in range(count):
        copy(n).start()

    place = lax.axis_index("clus").astype(jnp.int32)
    small[0].wait()
    small[1].wait()
    lower = tri_ref[...]
    eye = iota((ck, ck), 0) == iota((ck, ck), 1)
    scale = 1.0 / jnp.sum(jnp.where(eye, lower, 0.0), axis=1, keepdims=True)
    below = jnp.where(iota((ck, ck), 0) > iota((ck, ck), 1), lower * scale, 0.0)
    order = iota((ck, lanes), 0)
    order = order // rows * rows + order % modes * sub + order % rows // modes
    sol = jnp.where(iota((ck, lanes), 1) == rhs + order, scale, 0.0)
    for i in range(ck - 1):
        sol = sol - below[:, i : i + 1] * sol[i : i + 1, :]
    inv_ref[...] = sol
    wanted = iota((rows, ck), 1) == place * rows + iota((rows, ck), 0)
    own_map = jnp.sum(jnp.where(wanted, row_ref[...].astype(F32), 0.0), axis=1, keepdims=True)
    for c in range(lanes // LANES):
        cols = slice(c * LANES, (c + 1) * LANES)
        sol_ref[c] = sol[:, cols]
        block_ref[:, cols] = sol_ref[c, pl.ds(place * rows, rows), :]
    block_ref[...] += jnp.where(iota((rows, lanes), 1) == rhs + ck, own_map, 0.0)

    for one in small[2:]:
        one.wait()
    masked = mask_kernel(raw_ref, count_s, size_s, sub)
    for n in range(count):
        x_ref[n, flat:, :] = jnp.zeros((deep - flat, step), BF16)
        x_ref[n, flat : flat + rows, :] = masked[:, n * step : (n + 1) * step]
    acc_ref[...] = jnp.zeros_like(acc_ref)
    cut = up(rhs * sub // 2, 16)
    halves = [(0, cut), (cut, rhs * sub)]
    sums = [jnp.zeros((rows, stop - start), F32) for start, stop in halves]
    for n in range(count):
        copy(n).wait()
        weight = masked[:, n * step : (n + 1) * step]
        sums = [part + dot(weight, x_ref[n, start:stop, :], NT) for part, (start, stop) in zip(sums, halves)]
    total = jnp.concatenate(sums, axis=1)
    same = iota((rows, rhs * sub), 0) % sub == iota((rows, rhs * sub), 1) % sub
    acc_ref[:rows, :] = jnp.where(same, total, 0.0)
    mixed = dot_exact(acc_ref[...], rows_of_slots(sub, rhs, lanes), NN)
    block = block_ref[...] + mixed[:rows, :]
    group = 2 if send_ref.shape[0] % (2 * rows) == 0 else 1
    block = jnp.concatenate([block] * group, axis=0)
    for d in range(send_ref.shape[0] // (rows * group)):
        send_ref[pl.ds(d * rows * group, rows * group), :] = block


def middle_kernel(rhs, rows, inv_ref, picked_ref, coarse_ref, turned_ref, turn_ref, own_ref=None):
    ck = picked_ref.shape[0]
    place = lax.axis_index("clus").astype(jnp.int32)
    turn_ref[...] = inv_ref[:, rhs : rhs + ck].T
    turned_ref[...] = jnp.zeros_like(turned_ref)
    turned_ref[:rows, :] = turn_ref[pl.ds(place * rows, rows), :]
    coarse_ref[...] = lax.dot_general(turned_ref[...], picked_ref[...], NN, precision=HI, preferred_element_type=F32)
    if own_ref is not None:
        cluster = lax.axis_index("wide").astype(jnp.int32)
        for w in range(own_ref.shape[1] // ck):
            own_ref[:, w * ck : (w + 1) * ck] = jnp.where(w == cluster, turned_ref[...], 0.0)


def middle_kernel_small(rhs, rows, inv_ref, picked_ref, coarse_ref, own_ref, turn_ref, turned_ref):
    middle_kernel(rhs, rows, inv_ref, picked_ref, coarse_ref, turned_ref, turn_ref, own_ref)


def write_out(corr, sub, x_ref, out_ref, corr_ref, o_ref, sems):
    flat, rhs = o_ref.shape[1], corr_ref.shape[1]
    count, deep, step = x_ref.shape
    base = flat // LANES * LANES
    corr_ref[: flat - base, :] = jnp.zeros((flat - base, rhs), BF16)
    corr_ref[flat - base :, :] = -corr
    wide = dot(rows_of_slots(sub, rhs, rhs), corr_ref[...], NT)
    row, col = iota(wide.shape, 0), iota(wide.shape, 1) + base
    same = (col >= flat) & (row % sub == col % sub)
    left = jnp.where(same, wide, (row == col).astype(F32)).astype(BF16)
    if base:
        eye = (iota((flat, base), 0) == iota((flat, base), 1)).astype(F32).astype(BF16)
        left = jnp.concatenate([eye, left], axis=1)
    tile = tile_of(step)
    out_flat = out_ref.reshape(flat, count * step)

    def copy(n, cols):
        part = out_flat.at[:, pl.ds(n * step + cols.start, tile)]
        return pltpu.make_async_copy(o_ref.at[n, :, cols], part, sems.at[n, cols.start // tile])

    tiles = [(n, slice(c, c + tile)) for n in range(count) for c in range(0, step, tile)]
    waiting = []
    for n, cols in [*tiles, *[(None, None)] * AHEAD]:
        if n is not None:
            waiting.append((n, cols, dot(left, x_ref[n, :, cols], NN)))
        if len(waiting) > AHEAD or n is None and waiting:
            done, where, value = waiting.pop(0)
            o_ref[done, :, where] = value.astype(BF16)
            copy(done, where).start()
    for n, cols in tiles:
        copy(n, cols).wait()


def block_product(recv_ref, rhs, ck, block_ref):
    total = recv_ref.shape[0]
    block_ref[...] = jnp.zeros_like(block_ref)
    for w in range(total // ck):
        here = slice(w * ck, (w + 1) * ck)
        block_ref[here, here] = recv_ref[here, rhs : rhs + ck]
    spans = []
    for start in range(0, total, LANES):
        stop = min(start + LANES, total)
        low = start // ck * ck // 16 * 16
        high = min(up(up(stop, ck), 16), total)
        spans.append((low, high, dot_parts(block_ref[low:high, start:stop], recv_ref[start:stop, :rhs], NN)))
    return spans


def last_kernel(rhs, sub, ck, recv_ref, coarse_ref, own_ref, x_ref, out_ref, block_ref, sum_ref, corr_ref, o_ref, sems):
    total = recv_ref.shape[0]
    gk = coarse_ref.shape[1]
    done = 0
    for low, high, part in block_product(recv_ref, rhs, ck, block_ref):
        if low < done:
            sum_ref[low:done, :] += part[: done - low]
        sum_ref[done:high, :] = part[done - low :]
        done = high
    target = recv_ref[:, rhs + ck : rhs + ck + 1].astype(jnp.int32)
    hot = (target == iota((total, gk), 1)).astype(F32).astype(BF16)
    taken = dot_exact(coarse_ref[...], hot, NT)
    corr = dot_parts(own_ref[...] - taken, sum_ref[...], NN)
    write_out(corr.astype(BF16), sub, x_ref, out_ref, corr_ref, o_ref, sems)


def last_kernel_plain(sub, given_ref, x_ref, out_ref, corr_ref, o_ref, sems):
    write_out(given_ref[...].astype(BF16), sub, x_ref, out_ref, corr_ref, o_ref, sems)


def per_device(duals, kernel, sub_counts, dual_sizes, cluster_factor, coarse_map, coarse_inverse):
    rhs, sub, width = duals.shape
    modes = kernel.shape[1]
    rows = sub * modes
    padded = up(rows, 16)
    clusters = lax.axis_size("wide")
    members = lax.axis_size("clus")
    devices = clusters * members
    total = devices * rows
    ck = cluster_factor.shape[1]
    gk, own_cols = coarse_inverse.shape
    lanes = up(rhs + ck + 1, LANES)
    count = chunks_of(width)
    step = width // count
    place = lax.axis_index("clus").astype(jnp.int32)
    counts = sub_counts.reshape(1, 1)
    sizes = stay(dual_sizes)
    modes_first = stay(kernel.transpose(1, 0, 2))
    vectors = stay(duals)
    slabs = (count, rhs * sub, step)
    deeper = (count, rhs * sub + padded, step)
    small_enough = total * max(total, gk) <= 2**20
    OUT = pltpu.VMEM if small_enough else jax.ShapeDtypeStruct

    send, inv, x = pl.pallas_call(
        functools.partial(first_kernel, rhs),
        out_shape=(jax.ShapeDtypeStruct((total, lanes), F32), OUT((ck, lanes), F32), OUT(deeper, BF16)),
        in_specs=[HBM] * 6,
        out_specs=(VMEM, VMEM, VMEM),
        scratch_shapes=[
            pltpu.SMEM((1, 1), jnp.int32),
            pltpu.SMEM((sub,), jnp.int32),
            pltpu.VMEM((rows, width), BF16),
            pltpu.VMEM((ck, ck), F32),
            pltpu.VMEM((1, ck), jnp.int32),
            pltpu.VMEM((padded, rhs * sub), F32),
            pltpu.VMEM((rows, lanes), F32),
            pltpu.VMEM((lanes // LANES, ck, LANES), F32),
            pltpu.SemaphoreType.DMA((count,)),
            pltpu.SemaphoreType.DMA((5,)),
        ],
        compiler_params=pltpu.CompilerParams(vmem_limit_bytes=FIRST_LIMIT),
    )(counts, sizes, modes_first, stay(cluster_factor[0]), stay(coarse_map), vectors)

    spread = send.reshape(devices, rows, lanes // LANES, LANES)
    recv = lax.all_to_all(spread, ("wide", "clus"), 0, 0)

    inv, rows_map, coarse_t, _ = lax.optimization_barrier((inv, coarse_map[0], coarse_inverse.T, send))
    hot = (rows_map[:, None] == place * own_cols + iota((ck, own_cols), 1)).astype(F32)
    part = jnp.dot(hot, coarse_t, precision=HI)
    picked = part
    for shift in range(1, members):
        picked = picked + lax.ppermute(part, "clus", [(i, (i + shift) % members) for i in range(members)])
    params = pltpu.CompilerParams(vmem_limit_bytes=LAST_LIMIT)
    coarse, turned = pl.pallas_call(
        functools.partial(middle_kernel_small if small_enough else middle_kernel, rhs, rows),
        out_shape=(OUT((padded, gk), F32), OUT((padded, total if small_enough else ck), F32)),
        in_specs=[VMEM, VMEM],
        out_specs=(VMEM, VMEM),
        scratch_shapes=[pltpu.VMEM((ck, ck), F32), pltpu.VMEM((padded, ck), F32)][: 1 + small_enough],
        compiler_params=params,
    )(inv, picked)

    out_shape = jax.ShapeDtypeStruct(duals.shape, BF16)
    scratch = [
        pltpu.VMEM((rhs * sub % LANES + padded, rhs), BF16),
        pltpu.VMEM(slabs, BF16),
        pltpu.SemaphoreType.DMA((count, step // tile_of(step))),
    ]
    if small_enough:
        return pl.pallas_call(
            functools.partial(last_kernel, rhs, sub, ck),
            out_shape=out_shape,
            in_specs=[VMEM] * 4,
            out_specs=HBM,
            scratch_shapes=[pltpu.VMEM((total, total), F32), pltpu.VMEM((total, rhs), F32), *scratch],
            compiler_params=params,
        )(recv.reshape(total, lanes), coarse, turned, x)

    blocks = recv.reshape(clusters, ck, lanes)
    forward = jnp.einsum("wam,wmr->war", blocks[:, :, rhs : rhs + ck], blocks[:, :, :rhs], precision=HI)
    target = blocks[:, :, rhs + ck].astype(jnp.int32).reshape(total)
    all_hot = (target[:, None] == iota((total, gk), 1)).astype(F32)
    gsum = lax.dot_general(all_hot, forward.reshape(total, rhs), (((0,), (0,)), ((), ())), precision=HI)
    mine = lax.dynamic_index_in_dim(forward, lax.axis_index("wide"), 0, keepdims=False)
    corr = jnp.dot(turned, mine, precision=HI) - jnp.dot(coarse, gsum, precision=HI)
    return pl.pallas_call(
        functools.partial(last_kernel_plain, sub),
        out_shape=out_shape,
        in_specs=[VMEM] * 2,
        out_specs=HBM,
        scratch_shapes=scratch,
        compiler_params=params,
    )(corr, x)


def solution(mesh):
    in_specs = (
        P(None, ("wide", "clus"), None),
        P(("wide", "clus"), None, None),
        P(("wide", "clus")),
        P(("wide", "clus")),
        P("wide", None, None),
        P("wide", None),
        P(None, "clus"),
    )
    out_specs = P(None, ("wide", "clus"), None)
    return jax.shard_map(
        per_device, mesh=mesh, in_specs=in_specs, out_specs=out_specs, check_vma=False
    )
```

```python
import functools

import jax
import jax.numpy as jnp
from jax import lax
from jax.experimental import pallas as pl
from jax.experimental.pallas import tpu as pltpu
from jax.sharding import PartitionSpec as P

F32 = jnp.float32
BF16 = jnp.bfloat16
LANES = 128
HI = lax.Precision.HIGHEST
NT = (((1,), (1,)), ((), ()))
NN = (((1,), (0,)), ((), ()))
VMEM = pl.BlockSpec(memory_space=pltpu.VMEM)
HBM = pl.BlockSpec(memory_space=pltpu.HBM)
FIRST_LIMIT = 60 * 2**20
LAST_LIMIT = 20 * 2**20
AHEAD = 6


def iota(shape, dim):
    return lax.broadcasted_iota(jnp.int32, shape, dim)


def stay(x):
    return pltpu.with_memory_space_constraint(x, pltpu.HBM)


def up(value, step):
    return -(-value // step) * step


def split(x, parts):
    out = []
    for n in range(parts):
        head = x.astype(BF16)
        out.append(head)
        if n + 1 < parts:
            x = x - head.astype(F32)
    return out


def dot(a, b, dims):
    return lax.dot_general(a, b, dims, preferred_element_type=F32)


def dot_parts(a, b, dims):
    a_hi, a_lo = split(a, 2)
    b_hi, b_lo = split(b, 2)
    rows = a.shape[0]
    both = dot(jnp.concatenate([a_hi, a_lo], axis=0), b_hi, dims)
    return both[:rows] + both[rows:] + dot(a_hi, b_lo, dims)


def dot_exact(a, hot, dims):
    rows = a.shape[0]
    parts = dot(jnp.concatenate(split(a, 3), axis=0), hot, dims)
    return parts[:rows] + parts[rows : 2 * rows] + parts[2 * rows :]


def chunks_of(width):
    for count in (5, 3, 2):
        if width % (count * LANES) == 0:
            return count
    return 1


def tile_of(step):
    return 2 * LANES if step % (2 * LANES) == 0 else LANES


def rows_of_slots(sub, rhs, lanes):
    return (iota((rhs * sub, lanes), 0) // sub == iota((rhs * sub, lanes), 1)).astype(F32).astype(BF16)


def slab_copies(whole_ref, slabs_ref, sems):
    count, _, step = slabs_ref.shape
    rows = whole_ref.shape[0] * whole_ref.shape[1]
    flat = whole_ref.reshape(rows, count * step)

    def copy(n):
        part = flat.at[:, pl.ds(n * step, step)]
        return pltpu.make_async_copy(part, slabs_ref.at[n, pl.ds(0, rows)], sems.at[n])

    return copy


def mask_kernel(raw_ref, count_s, size_s, sub):
    rows, width = raw_ref.shape
    slot = iota((rows, width), 0) % sub
    limit = jnp.zeros((rows, width), jnp.int32)
    for s in range(sub):
        size = jnp.where(s < count_s[0, 0], size_s[s], 0)
        limit = jnp.where(slot == s, size, limit)
    return jnp.where(iota((rows, width), 1) < limit, raw_ref[...].astype(F32), 0.0).astype(BF16)


def first_kernel(rhs, counts_ref, sizes_ref, kernel_ref, lower_ref, map_ref, duals_ref,
                 send_ref, inv_ref, x_ref,
                 count_s, size_s, raw_ref, tri_ref, row_ref, acc_ref, block_ref, sol_ref, sems, small_sems):
    modes, sub, width = kernel_ref.shape
    rows = modes * sub
    ck = lower_ref.shape[0]
    lanes = inv_ref.shape[1]
    count, deep, step = x_ref.shape
    flat = rhs * sub
    copy = slab_copies(duals_ref, x_ref, sems)
    small = [
        pltpu.make_async_copy(src, dst, small_sems.at[n])
        for n, (src, dst) in enumerate(
            (
                (lower_ref, tri_ref),
                (map_ref, row_ref),
                (counts_ref, count_s),
                (sizes_ref, size_s),
                (kernel_ref.reshape(rows, width), raw_ref),
            )
        )
    ]
    for one in small:
        one.start()
    for n in range(count):
        copy(n).start()

    place = lax.axis_index("clus").astype(jnp.int32)
    small[0].wait()
    small[1].wait()
    lower = tri_ref[...]
    eye = iota((ck, ck), 0) == iota((ck, ck), 1)
    scale = 1.0 / jnp.sum(jnp.where(eye, lower, 0.0), axis=1, keepdims=True)
    below = jnp.where(iota((ck, ck), 0) > iota((ck, ck), 1), lower * scale, 0.0)
    order = iota((ck, lanes), 0)
    order = order // rows * rows + order % modes * sub + order % rows // modes
    sol = jnp.where(iota((ck, lanes), 1) == rhs + order, scale, 0.0)
    for i in range(ck - 1):
        sol = sol - below[:, i : i + 1] * sol[i : i + 1, :]
    inv_ref[...] = sol
    wanted = iota((rows, ck), 1) == place * rows + iota((rows, ck), 0)
    own_map = jnp.sum(jnp.where(wanted, row_ref[...].astype(F32), 0.0), axis=1, keepdims=True)
    for c in range(lanes // LANES):
        cols = slice(c * LANES, (c + 1) * LANES)
        sol_ref[c] = sol[:, cols]
        block_ref[:, cols] = sol_ref[c, pl.ds(place * rows, rows), :]
    block_ref[...] += jnp.where(iota((rows, lanes), 1) == rhs + ck, own_map, 0.0)

    for one in small[2:]:
        one.wait()
    masked = mask_kernel(raw_ref, count_s, size_s, sub)
    for n in range(count):
        x_ref[n, flat:, :] = jnp.zeros((deep - flat, step), BF16)
        x_ref[n, flat : flat + rows, :] = masked[:, n * step : (n + 1) * step]
    acc_ref[...] = jnp.zeros_like(acc_ref)
    cut = up(rhs * sub // 2, 16)
    halves = [(0, cut), (cut, rhs * sub)]
    sums = [jnp.zeros((rows, stop - start), F32) for start, stop in halves]
    for n in range(count):
        copy(n).wait()
        weight = masked[:, n * step : (n + 1) * step]
        sums = [part + dot(weight, x_ref[n, start:stop, :], NT) for part, (start, stop) in zip(sums, halves)]
    total = jnp.concatenate(sums, axis=1)
    same = iota((rows, rhs * sub), 0) % sub == iota((rows, rhs * sub), 1) % sub
    acc_ref[:rows, :] = jnp.where(same, total, 0.0)
    mixed = dot_exact(acc_ref[...], rows_of_slots(sub, rhs, lanes), NN)
    block = block_ref[...] + mixed[:rows, :]
    group = 2 if send_ref.shape[0] % (2 * rows) == 0 else 1
    block = jnp.concatenate([block] * group, axis=0)
    for d in range(send_ref.shape[0] // (rows * group)):
        send_ref[pl.ds(d * rows * group, rows * group), :] = block


def middle_kernel(rhs, rows, inv_ref, picked_ref, coarse_ref, turned_ref, turn_ref, own_ref=None):
    ck = picked_ref.shape[0]
    place = lax.axis_index("clus").astype(jnp.int32)
    turn_ref[...] = inv_ref[:, rhs : rhs + ck].T
    turned_ref[...] = jnp.zeros_like(turned_ref)
    turned_ref[:rows, :] = turn_ref[pl.ds(place * rows, rows), :]
    coarse_ref[...] = lax.dot_general(turned_ref[...], picked_ref[...], NN, precision=HI, preferred_element_type=F32)
    if own_ref is not None:
        cluster = lax.axis_index("wide").astype(jnp.int32)
        for w in range(own_ref.shape[1] // ck):
            own_ref[:, w * ck : (w + 1) * ck] = jnp.where(w == cluster, turned_ref[...], 0.0)


def middle_kernel_small(rhs, rows, inv_ref, picked_ref, coarse_ref, own_ref, turn_ref, turned_ref):
    middle_kernel(rhs, rows, inv_ref, picked_ref, coarse_ref, turned_ref, turn_ref, own_ref)


def write_out(corr, sub, x_ref, out_ref, corr_ref, o_ref, sems):
    flat, rhs = o_ref.shape[1], corr_ref.shape[1]
    count, deep, step = x_ref.shape
    base = flat // LANES * LANES
    corr_ref[: flat - base, :] = jnp.zeros((flat - base, rhs), BF16)
    corr_ref[flat - base :, :] = -corr
    wide = dot(rows_of_slots(sub, rhs, rhs), corr_ref[...], NT)
    row, col = iota(wide.shape, 0), iota(wide.shape, 1) + base
    same = (col >= flat) & (row % sub == col % sub)
    left = jnp.where(same, wide, (row == col).astype(F32)).astype(BF16)
    if base:
        eye = (iota((flat, base), 0) == iota((flat, base), 1)).astype(F32).astype(BF16)
        left = jnp.concatenate([eye, left], axis=1)
    tile = tile_of(step)
    out_flat = out_ref.reshape(flat, count * step)

    def copy(n, cols):
        part = out_flat.at[:, pl.ds(n * step + cols.start, tile)]
        return pltpu.make_async_copy(o_ref.at[n, :, cols], part, sems.at[n, cols.start // tile])

    tiles = [(n, slice(c, c + tile)) for n in range(count) for c in range(0, step, tile)]
    waiting = []
    for n, cols in [*tiles, *[(None, None)] * AHEAD]:
        if n is not None:
            waiting.append((n, cols, dot(left, x_ref[n, :, cols], NN)))
        if len(waiting) > AHEAD or n is None and waiting:
            done, where, value = waiting.pop(0)
            o_ref[done, :, where] = value.astype(BF16)
            copy(done, where).start()
    for n, cols in tiles:
        copy(n, cols).wait()


def block_product(recv_ref, rhs, ck, block_ref):
    total = recv_ref.shape[0]
    bounds = []
    for start in range(0, total, LANES):
        stop = min(start + LANES, total)
        bounds.append((start, stop, start // ck * ck // 16 * 16, min(up(up(stop, ck), 16), total)))
    for start, stop, low, high in bounds:
        block_ref[low:high, start:stop] = jnp.zeros((high - low, stop - start), F32)
    for w in range(total // ck):
        here = slice(w * ck, (w + 1) * ck)
        block_ref[here, here] = recv_ref[here, rhs : rhs + ck]
    spans = []
    for start, stop, low, high in bounds:
        spans.append((low, high, dot_parts(block_ref[low:high, start:stop], recv_ref[start:stop, :rhs], NN)))
    return spans


def last_kernel(rhs, sub, ck, recv_ref, coarse_ref, own_ref, x_ref, out_ref, block_ref, sum_ref, corr_ref, o_ref, sems):
    total = recv_ref.shape[0]
    gk = coarse_ref.shape[1]
    done = 0
    for low, high, part in block_product(recv_ref, rhs, ck, block_ref):
        if low < done:
            sum_ref[low:done, :] += part[: done - low]
        sum_ref[done:high, :] = part[done - low :]
        done = high
    target = recv_ref[:, rhs + ck : rhs + ck + 1].astype(jnp.int32)
    hot = (target == iota((total, gk), 1)).astype(F32).astype(BF16)
    taken = dot_exact(coarse_ref[...], hot, NT)
    corr = dot_parts(own_ref[...] - taken, sum_ref[...], NN)
    write_out(corr.astype(BF16), sub, x_ref, out_ref, corr_ref, o_ref, sems)


def last_kernel_plain(sub, given_ref, x_ref, out_ref, corr_ref, o_ref, sems):
    write_out(given_ref[...].astype(BF16), sub, x_ref, out_ref, corr_ref, o_ref, sems)


def per_device(duals, kernel, sub_counts, dual_sizes, cluster_factor, coarse_map, coarse_inverse):
    rhs, sub, width = duals.shape
    modes = kernel.shape[1]
    rows = sub * modes
    padded = up(rows, 16)
    clusters = lax.axis_size("wide")
    members = lax.axis_size("clus")
    devices = clusters * members
    total = devices * rows
    ck = cluster_factor.shape[1]
    gk, own_cols = coarse_inverse.shape
    lanes = up(rhs + ck + 1, LANES)
    count = chunks_of(width)
    step = width // count
    place = lax.axis_index("clus").astype(jnp.int32)
    counts = sub_counts.reshape(1, 1)
    sizes = stay(dual_sizes)
    modes_first = stay(kernel.transpose(1, 0, 2))
    vectors = stay(duals)
    slabs = (count, rhs * sub, step)
    deeper = (count, rhs * sub + padded, step)
    small_enough = total * max(total, gk) <= 2**20
    OUT = pltpu.VMEM if small_enough else jax.ShapeDtypeStruct

    send, inv, x = pl.pallas_call(
        functools.partial(first_kernel, rhs),
        out_shape=(jax.ShapeDtypeStruct((total, lanes), F32), OUT((ck, lanes), F32), OUT(deeper, BF16)),
        in_specs=[HBM] * 6,
        out_specs=(VMEM, VMEM, VMEM),
        scratch_shapes=[
            pltpu.SMEM((1, 1), jnp.int32),
            pltpu.SMEM((sub,), jnp.int32),
            pltpu.VMEM((rows, width), BF16),
            pltpu.VMEM((ck, ck), F32),
            pltpu.VMEM((1, ck), jnp.int32),
            pltpu.VMEM((padded, rhs * sub), F32),
            pltpu.VMEM((rows, lanes), F32),
            pltpu.VMEM((lanes // LANES, ck, LANES), F32),
            pltpu.SemaphoreType.DMA((count,)),
            pltpu.SemaphoreType.DMA((5,)),
        ],
        compiler_params=pltpu.CompilerParams(vmem_limit_bytes=FIRST_LIMIT),
    )(counts, sizes, modes_first, stay(cluster_factor[0]), stay(coarse_map), vectors)

    spread = send.reshape(devices, rows, lanes // LANES, LANES)
    recv = lax.all_to_all(spread, ("wide", "clus"), 0, 0)

    inv, rows_map, coarse_t, _ = lax.optimization_barrier((inv, coarse_map[0], coarse_inverse.T, send))
    hot = (rows_map[:, None] == place * own_cols + iota((ck, own_cols), 1)).astype(F32)
    part = jnp.dot(hot, coarse_t, precision=HI)
    picked = part
    for shift in range(1, members):
        picked = picked + lax.ppermute(part, "clus", [(i, (i + shift) % members) for i in range(members)])
    params = pltpu.CompilerParams(vmem_limit_bytes=LAST_LIMIT)
    coarse, turned = pl.pallas_call(
        functools.partial(middle_kernel_small if small_enough else middle_kernel, rhs, rows),
        out_shape=(OUT((padded, gk), F32), OUT((padded, total if small_enough else ck), F32)),
        in_specs=[VMEM, VMEM],
        out_specs=(VMEM, VMEM),
        scratch_shapes=[pltpu.VMEM((ck, ck), F32), pltpu.VMEM((padded, ck), F32)][: 1 + small_enough],
        compiler_params=params,
    )(inv, picked)

    out_shape = jax.ShapeDtypeStruct(duals.shape, BF16)
    scratch = [
        pltpu.VMEM((rhs * sub % LANES + padded, rhs), BF16),
        pltpu.VMEM(slabs, BF16),
        pltpu.SemaphoreType.DMA((count, step // tile_of(step))),
    ]
    if small_enough:
        return pl.pallas_call(
            functools.partial(last_kernel, rhs, sub, ck),
            out_shape=out_shape,
            in_specs=[VMEM] * 4,
            out_specs=HBM,
            scratch_shapes=[pltpu.VMEM((total, total), F32), pltpu.VMEM((total, rhs), F32), *scratch],
            compiler_params=params,
        )(recv.reshape(total, lanes), coarse, turned, x)

    blocks = recv.reshape(clusters, ck, lanes)
    forward = jnp.einsum("wam,wmr->war", blocks[:, :, rhs : rhs + ck], blocks[:, :, :rhs], precision=HI)
    target = blocks[:, :, rhs + ck].astype(jnp.int32).reshape(total)
    all_hot = (target[:, None] == iota((total, gk), 1)).astype(F32)
    gsum = lax.dot_general(all_hot, forward.reshape(total, rhs), (((0,), (0,)), ((), ())), precision=HI)
    mine = lax.dynamic_index_in_dim(forward, lax.axis_index("wide"), 0, keepdims=False)
    corr = jnp.dot(turned, mine, precision=HI) - jnp.dot(coarse, gsum, precision=HI)
    return pl.pallas_call(
        functools.partial(last_kernel_plain, sub),
        out_shape=out_shape,
        in_specs=[VMEM] * 2,
        out_specs=HBM,
        scratch_shapes=scratch,
        compiler_params=params,
    )(corr, x)


def solution(mesh):
    in_specs = (
        P(None, ("wide", "clus"), None),
        P(("wide", "clus"), None, None),
        P(("wide", "clus")),
        P(("wide", "clus")),
        P("wide", None, None),
        P("wide", None),
        P(None, "clus"),
    )
    out_specs = P(None, ("wide", "clus"), None)
    return jax.shard_map(
        per_device, mesh=mesh, in_specs=in_specs, out_specs=out_specs, check_vma=False
    )
```
